256 devices in a mesh: seq: 64 (over z, y, core), tp: 4 (over x).
Axes of the slice: x: 4, y: 4, z: 8, core: 2. Of those that a mesh axis runs over, the one named last changes fastest.
Arguments:
- db_tokens: int32 [32768, 128], P('seq'), may hold values from 0 to 16383
- db_parent: int32 [32768, 128], P('seq'), may hold values from 0 to 126, as said below
- db_depth: int32 [32768, 128], P('seq'), may hold values from 0 to 31, as said below
- nb_rows: int32 [512, 2], P('seq'), may hold values from 0 to 32767, as said below
- seq_start: int32 [512], P('seq'), may hold values 0 or 1
- table: bfloat16 [16384, 1024], P(None, 'tp'), may hold values from -40 to 40
- depth_table: bfloat16 [32, 1024], P(None, 'tp'), may hold values from -3 to 3
- enc_gain: float32 [1024], replicated, may hold values from 0.25 to 1.75
- enc_qkv: bfloat16 [1024, 3, 1024], P('seq', None, 'tp'), may hold values from -0.1875 to 0.1875
- tree_bias: float32 [8], replicated, may hold values from 1 to 4
- enc_wo: bfloat16 [1024, 1024], P('tp', 'seq'), may hold values from -0.1875 to 0.1875
- cond_kv: bfloat16 [32768, 2, 1024], P('seq', None, 'tp'), may hold values from -150 to 150
- queries: bfloat16 [32768, 4096], P('seq', 'tp'), may hold values from -150 to 150
- cca_kv: bfloat16 [1024, 2, 512], P('seq', None, 'tp'), may hold values from -0.1875 to 0.1875
Outputs:
- attended: bfloat16 [32768, 4096], P('seq', 'tp')
The draws below stay inside these ranges and needn't reach their ends.
Inputs may be any that keep to these rules, and one draw needn't show every extreme that they name: `db_parent`: position 0 of every stored neighbour is its own parent; every other position's parent is one of the three positions just before it. `db_depth`: position 0 has depth 0; every other position has its parent's depth plus one, capped at 31. `nb_rows`: rows 512 * i to 512 * (i + 1) - 1 of the database lie on index i of seq. Of the 16 neighbours of one index's blocks at most 1 lie on any one index; at most 32 neighbours of all blocks lie on one index, and in every draw some index holds exactly 32.
All inputs are finite; a program needn't handle non-finite values. No bound on the sum of `seq_start` on one device may be relied on, other than what follows from the above.
Results may differ from the reference program's by a relative error of at most 0.0223.
The reference program's roundings to bfloat16 on the way count: a program that leaves them out, or rounds other values in their place, can miss the bound.
Values may be sent and summed in bfloat16 or wider, within the bound.
No kernel may reach another device: no remote copies, remote signals or barrier semaphores. Data moves between devices by JAX's collectives and lax.ppermute only.
A program may use at most 128 MiB of HBM per device.

```python
import math
import jax
import jax.numpy as jnp
import numpy as np
from jax import lax

E = 1024
EH = 8
HD = 128
HQ = 32
KVH = 4
VOCAB = 16384
CL = 64
NL = 128
KN = 2
DEPTHS = 32
CH_DEV = 8
DB_DEV = 512
BLOCKS = 512
TOKENS = 32768
DB_ROWS = 32768
N_SEQ = 64


def tree_layout(key):
    steps_back = jax.random.randint(key, (DB_ROWS, NL), 1, 4)
    positions = jnp.arange(NL, dtype=jnp.int32)[None, :]
    parents = jnp.maximum(positions - steps_back, 0).astype(jnp.int32)

    def advance(column, depths):
        parent_col = lax.dynamic_slice_in_dim(parents, column, 1, 1)
        parent_depth = jnp.take_along_axis(depths, parent_col, axis=1)
        updated = jnp.minimum(parent_depth + 1, DEPTHS - 1).astype(jnp.int32)
        return lax.dynamic_update_slice_in_dim(depths, updated, column, 1)
    depths = lax.fori_loop(1, NL, advance, jnp.zeros((DB_ROWS, NL), jnp.int32))
    return (parents, depths)


def draw_db_parent(key, part):
    parents, depths = tree_layout(jax.random.fold_in(key, 11))
    return parents


def draw_db_depth(key, part):
    parents, depths = tree_layout(jax.random.fold_in(key, 11))
    return depths


def draw_nb_rows(key, part):
    subkeys = jax.random.split(jax.random.fold_in(key, 51), 4)
    per_device = KN * CH_DEV
    holders = jax.random.permutation(subkeys[0], N_SEQ)
    offset = jax.random.randint(subkeys[1], (), 0, N_SEQ)
    ordering = jax.vmap(lambda subkey: jax.random.permutation(subkey, per_device))(jax.random.split(subkeys[2], N_SEQ))
    source = jnp.arange(N_SEQ, dtype=jnp.int32)[:, None]
    virtual = (source + offset + ordering) % N_SEQ
    midway = N_SEQ // 2
    quarter = N_SEQ // 4
    position = jnp.where(virtual < midway, virtual, jnp.where(virtual < midway + quarter, virtual - midway, virtual))
    holder = holders[position]
    stored_row = jax.random.randint(subkeys[3], (N_SEQ, per_device), 0, DB_DEV)
    return (holder * DB_DEV + stored_row).reshape(BLOCKS, KN).astype(jnp.int32)


def draw_table(key, part):
    subkeys = jax.random.split(jax.random.fold_in(key, 21), 3)
    column_scale = jnp.exp(jax.random.uniform(subkeys[1], (1, E), jnp.float32, jnp.log(0.3), jnp.log(3.0)))
    row_scale = jnp.exp(jax.random.uniform(subkeys[2], (VOCAB, 1), jnp.float32, jnp.log(0.5), jnp.log(2.0)))
    base = jnp.clip(jax.random.normal(subkeys[0], (VOCAB, E), jnp.float32), -6.0, 6.0)
    return (base * column_scale * row_scale).astype(jnp.bfloat16)


def draw_cond_kv(key, part):
    subkeys = jax.random.split(jax.random.fold_in(key, 41), 1)
    base = jnp.clip(jax.random.normal(subkeys[0], (TOKENS, 2, E), jnp.float32), -6.0, 6.0)
    return base.astype(jnp.bfloat16)


def draw_queries(key, part):
    subkeys = jax.random.split(jax.random.fold_in(key, 31), 1)
    base = jnp.clip(jax.random.normal(subkeys[0], (TOKENS, HQ * HD), jnp.float32), -6.0, 6.0)
    return base.astype(jnp.bfloat16)


def set_ends(entries, rng, smallest, high):
    index_at = [jax.random.randint(jax.random.fold_in(rng, axis), (), 0, length) for axis, length in enumerate(entries.shape)]
    widest = entries.shape.index(max(entries.shape))
    neighbour = index_at[:widest] + [(index_at[widest] + 1) % entries.shape[widest]] + index_at[widest + 1:]
    return entries.at[tuple(index_at)].set(smallest).at[tuple(neighbour)].set(high)


def levels(rng, shape, pieces, low, top_value):
    loudness = 1.0
    for dim, parts in pieces:
        draws = jax.random.uniform(jax.random.fold_in(jax.random.fold_in(rng, 6), dim), (parts,), jnp.float32, low / len(pieces), top_value / len(pieces))
        loudness = loudness * jnp.repeat(jnp.exp(draws), shape[dim] // parts).reshape((-1,) + (1,) * (len(shape) - 1 - dim))
    return loudness


def rank_table(amount, slope):
    portions = [(1 << 20) // math.isqrt(standing ** slope) + 1 for standing in range(1, amount + 1)]
    spread = 1 + sum(portions) // (1 << 30)
    return np.cumsum(np.array([max(1, weight // spread) for weight in portions]))


def skewed_ids(stream_key, extent, count, lean):
    grid = rank_table(count, lean)
    pick = jax.random.randint(jax.random.fold_in(stream_key, 1), extent, 0, int(grid[count - 1]))
    standing = jnp.searchsorted(jnp.asarray(grid, jnp.int32), pick, side="right")
    return jax.random.permutation(jax.random.fold_in(stream_key, 2), count)[standing].astype(jnp.int32)


def noise(rng, extent, width, limit, cuts=(), held_as=jnp.bfloat16):
    drawn = width * jax.random.normal(rng, extent, jnp.float32)
    if cuts:
        drawn = drawn * levels(rng, extent, cuts, -0.22, 0.18)
    return jnp.clip(drawn, -limit, limit).astype(held_as)


def setup_inputs(seed: int = 0) -> dict:
    key_list = jax.random.split(jax.random.key(seed), 15)
    db_tokens = set_ends(skewed_ids(key_list[0], (DB_ROWS, NL), VOCAB, 2), jax.random.fold_in(key_list[0], 3), 0, VOCAB - 1).astype(jnp.int32)
    db_parent = draw_db_parent(jax.random.fold_in(key_list[14], 71), 0)
    db_depth = draw_db_depth(jax.random.fold_in(key_list[14], 71), 0)
    nb_rows = draw_nb_rows(jax.random.fold_in(key_list[14], 71), 0)
    seq_start = set_ends((jax.random.randint(key_list[4], (BLOCKS,), 0, 8) < 1).astype(jnp.int32), jax.random.fold_in(key_list[4], 1), 0, 1)
    table = draw_table(jax.random.fold_in(key_list[14], 71), 0)
    depth_table = noise(key_list[6], (DEPTHS, E), 0.5, 3.0, ((1, 4),))
    enc_gain = jnp.clip(1.0 + 0.15 * jax.random.normal(key_list[7], (E,), jnp.float32), 0.25, 1.75)
    enc_qkv = noise(key_list[8], (E, 3, E), E ** -0.5, 0.1875, ((0, 64), (2, 4)))
    tree_bias = jnp.clip(jax.random.uniform(key_list[9], (EH,), jnp.float32, 1.0, 4.0), 1.0, 4.0)
    enc_wo = noise(key_list[10], (E, E), E ** -0.5, 0.1875, ((0, 4), (1, 64)))
    cond_kv = draw_cond_kv(jax.random.fold_in(key_list[14], 71), 0)
    queries = draw_queries(jax.random.fold_in(key_list[14], 71), 0)
    cca_kv = noise(key_list[13], (E, 2, KVH * HD), E ** -0.5, 0.1875, ((0, 64), (2, 4)))
    return dict(db_tokens=db_tokens, db_parent=db_parent, db_depth=db_depth, nb_rows=nb_rows, seq_start=seq_start, table=table, depth_table=depth_table, enc_gain=enc_gain, enc_qkv=enc_qkv, tree_bias=tree_bias, enc_wo=enc_wo, cond_kv=cond_kv, queries=queries, cca_kv=cca_kv)


def rounded(values):
    return lax.optimization_barrier(values.astype(jnp.bfloat16)).astype(jnp.float32)

def reference(db_tokens, db_parent, db_depth, nb_rows, seq_start, table, depth_table, enc_gain, enc_qkv, tree_bias, enc_wo, cond_kv, queries, cca_kv):
    score_scale = 1.0 / math.sqrt(HD)
    qkv_weight = enc_qkv.astype(jnp.float32)
    out_weight = enc_wo.astype(jnp.float32)
    kv_weight = cca_kv.astype(jnp.float32)
    conditioning = cond_kv.reshape(BLOCKS, CL, 2, E)
    query_heads = queries.reshape(BLOCKS, CL, HQ, HD)
    positions = jnp.arange(NL, dtype=jnp.int32)

    def encode(row_pair, cond_block):
        tokens = db_tokens[row_pair]
        parents = db_parent[row_pair]
        depths = db_depth[row_pair]
        embedded = (table[tokens].astype(jnp.float32) + depth_table[depths].astype(jnp.float32)).astype(jnp.bfloat16)
        embedded_f = embedded.astype(jnp.float32)
        normed = rounded(embedded_f * lax.rsqrt(lax.optimization_barrier(jnp.mean(embedded_f * embedded_f, axis=-1, keepdims=True)) + 1e-05) * enc_gain)
        projected = rounded(jnp.einsum('kne,eaf->knaf', normed, qkv_weight))
        query_enc = projected[:, :, 0].reshape(KN, NL, EH, HD)
        key_enc = projected[:, :, 1].reshape(KN, NL, EH, HD)
        value_enc = projected[:, :, 2].reshape(KN, NL, EH, HD)
        cond_keys = cond_block[:, 0].astype(jnp.float32).reshape(CL, EH, HD)
        cond_values = cond_block[:, 1].astype(jnp.float32).reshape(CL, EH, HD)
        self_scores = jnp.einsum('kihd,kjhd->khij', query_enc, key_enc) * score_scale
        parent_hit = (parents[:, :, None] == positions[None, None, :]).astype(jnp.float32)
        self_scores = self_scores + tree_bias[None, :, None, None] * parent_hit[:, None, :, :]
        cond_scores = jnp.einsum('kihd,rhd->khir', query_enc, cond_keys) * score_scale
        weights = rounded(jax.nn.softmax(jnp.concatenate([self_scores, cond_scores], axis=-1), axis=-1))
        mixed = jnp.einsum('khij,kjhd->kihd', weights[..., :NL], value_enc) + jnp.einsum('khir,rhd->kihd', weights[..., NL:], cond_values)
        mixed = rounded(mixed.reshape(KN, NL, EH * HD))
        encoded = rounded(embedded_f + jnp.einsum('knf,fe->kne', mixed, out_weight))
        keys_values = rounded(jnp.einsum('kne,eaf->knaf', encoded, kv_weight))
        return keys_values.reshape(KN * NL, 2, KVH, HD)

    def attend(query, keys_values):
        grouped = query.reshape(query.shape[0], KVH, HQ // KVH, HD)
        scores = jnp.einsum('tkgd,pkd->kgtp', grouped, keys_values[:, 0]) * score_scale
        weights = rounded(jax.nn.softmax(scores, axis=-1))
        output = jnp.einsum('kgtp,pkd->tkgd', weights, keys_values[:, 1])
        return output.astype(jnp.bfloat16).reshape(query.shape[0], HQ * HD)

    def advance(carried, inputs):
        row_pair, cond_block, query_block, start_flag, block_index = inputs
        current = encode(row_pair, cond_block)
        query_f = query_block.astype(jnp.float32)
        leading = attend(query_f[:CL - 1], carried)
        allowed = (block_index > 0) & (start_flag == 0)
        leading = jnp.where(allowed, leading, jnp.zeros_like(leading))
        trailing = attend(query_f[CL - 1:], current)
        return (current, jnp.concatenate([leading, trailing], axis=0))
    initial = jnp.zeros((KN * NL, 2, KVH, HD), jnp.float32)
    final_state, attended = lax.scan(advance, initial, (nb_rows, conditioning, query_heads, seq_start, jnp.arange(BLOCKS, dtype=jnp.int32)))
    return attended.reshape(TOKENS, HQ * HD)
```

```python
import math

import jax
import jax.numpy as jnp
from jax import lax
from jax.sharding import PartitionSpec as P

HD = 128
SCALE = 1.0 / math.sqrt(HD)


def exchange(value, axis):
    return lax.all_to_all(value, axis, split_axis=0, concat_axis=0, tiled=True)


def normalize(embedded, gain):
    embedded_f = embedded.astype(jnp.float32)
    return (
        embedded_f
        * lax.rsqrt(jnp.mean(embedded_f * embedded_f, axis=-1, keepdims=True) + 1e-05)
        * gain
    ).astype(jnp.bfloat16)


def encoder_mix(normed, parents, cond_keys, cond_values, w_qkv, bias):
    unit_count, length, _ = normed.shape
    blocks, cond_len, head_count, _ = cond_keys.shape
    pair_count = unit_count // blocks
    projected = jnp.einsum(
        "une,eaf->unaf", normed, w_qkv, preferred_element_type=jnp.float32
    ).astype(jnp.bfloat16)
    shaped = projected.reshape(blocks, pair_count, length, 3, head_count, HD)
    query_part = shaped[:, :, :, 0]
    key_part = shaped[:, :, :, 1]
    value_part = shaped[:, :, :, 2]
    self_scores = (
        jnp.einsum("cpihd,cpjhd->cphij", query_part, key_part, preferred_element_type=jnp.float32)
        * SCALE
    )
    parent_hit = (
        parents.reshape(blocks, pair_count, length)[:, :, :, None]
        == jnp.arange(length, dtype=parents.dtype)[None, None, None, :]
    ).astype(jnp.float32)
    self_scores = self_scores + bias[None, None, :, None, None] * parent_hit[:, :, None]
    cond_scores = (
        jnp.einsum("cpihd,crhd->cphir", query_part, cond_keys, preferred_element_type=jnp.float32)
        * SCALE
    )
    weights = jax.nn.softmax(jnp.concatenate([self_scores, cond_scores], axis=-1), axis=-1).astype(
        jnp.bfloat16
    )
    mixed = jnp.einsum(
        "cphij,cpjhd->cpihd", weights[..., :length], value_part, preferred_element_type=jnp.float32
    )
    mixed = mixed + jnp.einsum(
        "cphir,crhd->cpihd", weights[..., length:], cond_values, preferred_element_type=jnp.float32
    )
    return mixed.astype(jnp.bfloat16).reshape(unit_count, length, head_count * HD)


def attend(query, key_value):
    blocks, key_rows = (key_value.shape[0], key_value.shape[1])
    token_count = query.shape[1]
    head_count = query.shape[2]
    kv_heads = key_value.shape[3] // HD
    group = head_count // kv_heads
    grouped = query.reshape(blocks, token_count, kv_heads, group, HD)
    key_part = key_value[:, :, 0].reshape(blocks, key_rows, kv_heads, HD)
    value_part = key_value[:, :, 1].reshape(blocks, key_rows, kv_heads, HD)
    scores = (
        jnp.einsum("ctkgd,cpkd->ckgtp", grouped, key_part, preferred_element_type=jnp.float32)
        * SCALE
    )
    weights = jax.nn.softmax(scores, axis=-1).astype(jnp.bfloat16)
    output = jnp.einsum(
        "ckgtp,cpkd->ctkgd", weights, value_part, preferred_element_type=jnp.float32
    ).astype(jnp.bfloat16)
    return output.reshape(blocks, token_count, head_count, HD)


def shards(
    db_tokens,
    db_parent,
    db_depth,
    nb_rows,
    seq_start,
    table,
    depth_table,
    enc_gain,
    enc_qkv,
    tree_bias,
    enc_wo,
    cond_kv,
    queries,
    cca_kv,
):
    seq_size = lax.axis_size("seq")
    tp_size = lax.axis_size("tp")
    block_count, pair_count = nb_rows.shape
    unit_count = block_count * pair_count
    stored, length = db_tokens.shape
    columns = table.shape[1]
    width = columns * tp_size
    rows_here = enc_qkv.shape[0]

    share = jnp.concatenate(
        [
            enc_qkv.transpose(1, 0, 2).reshape(3 * rows_here, columns),
            enc_wo.T,
            cca_kv.reshape(rows_here, columns),
        ],
        axis=0,
    )
    shares = lax.all_gather(share, ("seq", "tp"), axis=0).reshape(
        seq_size, tp_size, 5, rows_here, columns
    )
    w_qkv = (
        shares[:, :, :3].transpose(0, 3, 2, 1, 4).reshape(width, 3, width)
    )
    w_out = shares[:, :, 3].transpose(0, 2, 1, 3).reshape(width, width)
    kv_cols = cca_kv.shape[2]
    w_cca = (
        shares[:, :, 4]
        .reshape(seq_size, tp_size, rows_here, 2, kv_cols)
        .transpose(0, 2, 3, 1, 4)
        .reshape(width, 2, tp_size * kv_cols)
    )

    cond_len = cond_kv.shape[0] // block_count
    my_blocks = block_count // tp_size
    cond = exchange(
        cond_kv.reshape(tp_size, my_blocks * cond_len, 2 * columns), "tp"
    ).reshape(tp_size, my_blocks, cond_len, 2, columns // HD, HD)
    cond = cond.transpose(3, 1, 2, 0, 4, 5).reshape(2, my_blocks, cond_len, width // HD, HD)

    flat_rows = nb_rows.reshape(unit_count)
    holder = flat_rows // stored
    local_row = flat_rows % stored
    places = jnp.arange(seq_size, dtype=jnp.int32)
    request = jnp.sum(
        jnp.where(holder[None, :] == places[:, None], local_row[None, :], 0), axis=1
    )
    request = jnp.broadcast_to(request[:, None], (seq_size, 16))
    wanted = exchange(request, "seq")[:, 0]
    reply = jnp.concatenate(
        [
            jnp.take(db_tokens, wanted, axis=0),
            jnp.take(db_depth, wanted, axis=0),
            jnp.take(db_parent, wanted, axis=0),
        ],
        axis=1,
    )
    fetched = jnp.take(exchange(reply, "seq"), holder, axis=0)
    tokens = fetched[:, :length].reshape(unit_count * length)
    depths = fetched[:, length : 2 * length].reshape(unit_count * length)
    parents = fetched[:, 2 * length :]
    depth_hit = (
        depths[:, None] == jnp.arange(depth_table.shape[0], dtype=jnp.int32)[None, :]
    ).astype(jnp.bfloat16)
    embedded = (
        jnp.take(table, tokens, axis=0).astype(jnp.float32)
        + jnp.dot(depth_hit, depth_table, preferred_element_type=jnp.float32)
    ).astype(jnp.bfloat16)

    my_units = unit_count // tp_size
    pieces = exchange(embedded.reshape(tp_size, my_units * length, columns), "tp")
    embedded = pieces.transpose(1, 0, 2).reshape(my_units, length, width)
    parents = lax.dynamic_slice_in_dim(parents, lax.axis_index("tp") * my_units, my_units)
    normed = normalize(embedded, enc_gain)
    mixed = encoder_mix(normed, parents, cond[0], cond[1], w_qkv, tree_bias)
    increment = jnp.einsum("unf,ef->une", mixed, w_out, preferred_element_type=jnp.float32)
    encoded = (embedded.astype(jnp.float32) + increment).astype(jnp.bfloat16)
    keys_values = jnp.einsum(
        "une,eaf->unaf", encoded, w_cca, preferred_element_type=jnp.float32
    ).astype(jnp.bfloat16)
    outgoing = keys_values.reshape(my_units * length, 2, tp_size, kv_cols).transpose(2, 0, 1, 3)
    key_rows = pair_count * length
    keys_values = exchange(
        outgoing.reshape(tp_size, my_units * length, 2 * kv_cols), "tp"
    ).reshape(block_count, key_rows, 2, kv_cols)
    carried = lax.ppermute(
        keys_values[block_count - 1], "seq", [(s, s + 1) for s in range(seq_size - 1)]
    )
    previous = jnp.concatenate([carried[None], keys_values[: block_count - 1]], axis=0)
    head_queries = queries.shape[1] // HD
    query_heads = queries.reshape(block_count, cond_len, head_queries, HD)
    leading = attend(query_heads[:, : cond_len - 1], previous)
    trailing = attend(query_heads[:, cond_len - 1 :], keys_values)
    block_index = lax.axis_index("seq") * block_count + jnp.arange(block_count, dtype=jnp.int32)
    allowed = (block_index > 0) & (seq_start == 0)
    leading = jnp.where(allowed[:, None, None, None], leading, jnp.zeros_like(leading))
    attended = jnp.concatenate([leading, trailing], axis=1)
    return attended.reshape(block_count * cond_len, head_queries * HD)


def solution(mesh):
    in_specs = (
        P("seq", None),
        P("seq", None),
        P("seq", None),
        P("seq", None),
        P("seq"),
        P(None, "tp"),
        P(None, "tp"),
        P(),
        P("seq", None, "tp"),
        P(),
        P("tp", "seq"),
        P("seq", None, "tp"),
        P("seq", "tp"),
        P("seq", None, "tp"),
    )
    out_specs = P("seq", "tp")
    return jax.shard_map(shards, mesh=mesh, in_specs=in_specs, out_specs=out_specs, check_vma=False)
```

```python
import functools
import math

import jax
import jax.numpy as jnp
from jax import lax
from jax.experimental import pallas as pl
from jax.experimental.pallas import tpu as pltpu
from jax.sharding import PartitionSpec as P

HD = 128
SHARE = 16
SCALE = 1.0 / math.sqrt(HD)


def exchange(value, axis):
    return lax.all_to_all(value, axis, split_axis=0, concat_axis=0, tiled=True)


def assemble(refs, place_ref, target, first, count):
    for r, ref in enumerate(refs):
        slots = ref.shape[0]

        def copy(slot, carry, ref=ref, r=r):
            row = pl.multiple_of(place_ref[r, slot] * SHARE, SHARE)
            for a in range(count):
                target[first + a, pl.ds(row, SHARE), :] = ref[slot, pl.ds(a * SHARE, SHARE), :]
            return carry

        lax.fori_loop(0, slots, copy, 0, unroll=8)


def encoder_body(
    parts, my_units, length, cond_len, place_ref, xs_ref, bias_ref, emb_ref, gain_ref, hit_ref, cond_ref, *refs
):
    wa_refs, wo_refs, wc_refs = refs[:parts], refs[parts : 2 * parts], refs[2 * parts : 3 * parts]
    out_ref, normed_ref, acc_ref, enc_ref, mixed_ref, buf_ref = refs[3 * parts :]
    step = pl.program_id(0)
    pieces, rows, columns = emb_ref.shape
    width = pieces * columns
    nt = (((1,), (1,)), ((), ()))
    nn = (((1,), (0,)), ((), ()))

    @pl.when(step == 0)
    def _():
        for n in range(my_units):
            here = pl.ds(n * length, length)
            value = jnp.concatenate(
                [emb_ref[t, here, :].astype(jnp.float32) for t in range(pieces)], axis=1
            )
            acc_ref[here, :] = value
            mean = jnp.sum(value * value, axis=1, keepdims=True) * (1.0 / width)
            normed_ref[here, :] = (value * lax.rsqrt(mean + 1e-05) * gain_ref[...]).astype(jnp.bfloat16)

    @pl.when(step < pieces)
    def _():
        head = xs_ref[step] * (columns // HD)
        assemble(wa_refs, place_ref, buf_ref, 0, 3)
        assemble(wo_refs, place_ref, buf_ref, 3, 1)
        normed = normed_ref[...]
        project = lambda a: lax.dot_general(
            normed, buf_ref[a], nn, preferred_element_type=jnp.float32
        ).astype(jnp.bfloat16)
        query, key, value = project(0), project(1), project(2)
        for h in range(columns // HD):
            cols = slice(h * HD, (h + 1) * HD)
            bias = bias_ref[head + h]
            for n in range(my_units):
                here = slice(n * length, (n + 1) * length)
                block = n * length // (rows // (cond_ref.shape[1] // cond_len))
                cond_rows = pl.ds(block * cond_len, cond_len)
                q = query[here, cols]
                self_scores = lax.dot_general(
                    q, key[here, cols], nt, preferred_element_type=jnp.float32
                ) * SCALE + bias * hit_ref[here, :].astype(jnp.float32)
                cond_scores = (
                    lax.dot_general(
                        q,
                        cond_ref[0, cond_rows, pl.ds(h * HD, HD)],
                        nt,
                        preferred_element_type=jnp.float32,
                    )
                    * SCALE
                )
                top = jnp.maximum(
                    jnp.max(self_scores, axis=1, keepdims=True),
                    jnp.max(cond_scores, axis=1, keepdims=True),
                )
                self_e = jnp.exp(self_scores - top)
                cond_e = jnp.exp(cond_scores - top)
                inverse = 1.0 / (
                    jnp.sum(self_e, axis=1, keepdims=True) + jnp.sum(cond_e, axis=1, keepdims=True)
                )
                mixed = lax.dot_general(
                    (self_e * inverse).astype(jnp.bfloat16),
                    value[here, cols],
                    nn,
                    preferred_element_type=jnp.float32,
                ) + lax.dot_general(
                    (cond_e * inverse).astype(jnp.bfloat16),
                    cond_ref[0, cond_rows, pl.ds(columns + h * HD, HD)],
                    nn,
                    preferred_element_type=jnp.float32,
                )
                mixed_ref[here, cols] = mixed.astype(jnp.bfloat16)
        acc_ref[...] += lax.dot_general(
            mixed_ref[...], buf_ref[3], nt, preferred_element_type=jnp.float32
        )

    @pl.when(step == pieces)
    def _():
        enc_ref[...] = acc_ref[...].astype(jnp.bfloat16)

    @pl.when(step >= pieces)
    def _():
        assemble(wc_refs, place_ref, buf_ref, 4, 1)
        out_ref[0] = lax.dot_general(
            enc_ref[...], buf_ref[4], nn, preferred_element_type=jnp.float32
        ).astype(jnp.bfloat16)


def encoder(place, xs, bias, emb, gain, hit, cond, weights, x_dim, my_units, length, cond_len):
    pieces, rows, columns = emb.shape
    width = pieces * columns
    last = pieces - 1
    full = lambda shape: pl.BlockSpec(shape, lambda i, p, x: (0,) * len(shape))
    specs = {"a": [], "o": [], "c": []}
    arrays = {"a": [], "o": [], "c": []}
    for kind, array, height, index in weights:
        slots = array.shape[1 - x_dim]
        pick = (
            (lambda i: jnp.minimum(i, last)) if kind in "ao" else (lambda i: jnp.maximum(i - pieces, 0))
        )
        if x_dim == 0:
            shape = (None, slots, height, columns)
            mapping = lambda i, p, x, pick=pick, index=index: (pick(i), 0, index, 0)
        else:
            shape = (slots, None, height, columns)
            mapping = lambda i, p, x, pick=pick, index=index: (0, pick(i), index, 0)
        specs[kind].append(pl.BlockSpec(shape, mapping))
        arrays[kind].append(array)
    parts = len(specs["a"])
    return pl.pallas_call(
        functools.partial(encoder_body, parts, my_units, length, cond_len),
        out_shape=jax.ShapeDtypeStruct((pieces, rows, columns), jnp.bfloat16),
        grid_spec=pltpu.PrefetchScalarGridSpec(
            num_scalar_prefetch=2,
            grid=(2 * pieces,),
            in_specs=[
                pl.BlockSpec(memory_space=pltpu.SMEM),
                full(emb.shape),
                full(gain.shape),
                full(hit.shape),
                pl.BlockSpec(
                    (1,) + cond.shape[1:], lambda i, p, x: (x[jnp.minimum(i, last)], 0, 0)
                ),
                *specs["a"],
                *specs["o"],
                *specs["c"],
            ],
            out_specs=pl.BlockSpec(
                (1, rows, columns), lambda i, p, x: (x[jnp.maximum(i - pieces, 0)], 0, 0)
            ),
            scratch_shapes=[
                pltpu.VMEM((rows, width), jnp.bfloat16),
                pltpu.VMEM((rows, width), jnp.float32),
                pltpu.VMEM((rows, width), jnp.bfloat16),
                pltpu.VMEM((rows, columns), jnp.bfloat16),
                pltpu.VMEM((5, width, columns), jnp.bfloat16),
            ],
        ),
        compiler_params=pltpu.CompilerParams(
            dimension_semantics=("arbitrary",), vmem_limit_bytes=48 * 1024 * 1024
        ),
        name="encoder",
    )(place, xs, bias, emb, gain, hit, cond, *arrays["a"], *arrays["o"], *arrays["c"])


def attend_body(heads, allowed_ref, q_ref, cur_ref, prev_ref, carried_ref, out_ref):
    block = pl.program_id(0)
    nt = (((1,), (1,)), ((), ()))
    nn = (((1,), (0,)), ((), ()))
    tokens = q_ref.shape[0]
    previous = jnp.where(block == 0, carried_ref[...], prev_ref[...])

    def mix(query, kv):
        scores = (
            lax.dot_general(query, kv[:, :HD], nt, preferred_element_type=jnp.float32) * SCALE
        )
        e = jnp.exp(scores - jnp.max(scores, axis=1, keepdims=True))
        weights = (e * (1.0 / jnp.sum(e, axis=1, keepdims=True))).astype(jnp.bfloat16)
        return lax.dot_general(weights, kv[:, HD:], nn, preferred_element_type=jnp.float32)

    query = jnp.concatenate([q_ref[:, pl.ds(h * HD, HD)] for h in range(heads)], axis=0)
    leading = mix(query, previous)
    leading = jnp.where(allowed_ref[block] > 0, leading, jnp.zeros_like(leading))
    final = jnp.concatenate(
        [q_ref[tokens - 8 :, pl.ds(h * HD, HD)].astype(jnp.float32)[7:8] for h in range(heads)], axis=0
    ).astype(jnp.bfloat16)
    trailing = mix(final, cur_ref[...])
    row = lax.broadcasted_iota(jnp.int32, (tokens, HD), 0)
    for h in range(heads):
        out_ref[:, pl.ds(h * HD, HD)] = jnp.where(
            row == tokens - 1,
            jnp.broadcast_to(trailing[h : h + 1], (tokens, HD)),
            leading[h * tokens : (h + 1) * tokens],
        ).astype(jnp.bfloat16)


def attend(allowed, queries, keys_values, carried, key_rows):
    block_count = allowed.shape[0]
    tokens = queries.shape[0] // block_count
    heads = queries.shape[1] // HD
    return pl.pallas_call(
        functools.partial(attend_body, heads),
        out_shape=jax.ShapeDtypeStruct(queries.shape, jnp.bfloat16),
        grid=(block_count,),
        in_specs=[
            pl.BlockSpec(memory_space=pltpu.SMEM),
            pl.BlockSpec((tokens, queries.shape[1]), lambda c: (c, 0)),
            pl.BlockSpec((key_rows, 2 * HD), lambda c: (c, 0)),
            pl.BlockSpec((key_rows, 2 * HD), lambda c: (jnp.maximum(c - 1, 0), 0)),
            pl.BlockSpec((key_rows, 2 * HD), lambda c: (0, 0)),
        ],
        out_specs=pl.BlockSpec((tokens, queries.shape[1]), lambda c: (c, 0)),
        compiler_params=pltpu.CompilerParams(dimension_semantics=("arbitrary",)),
        name="attend",
    )(allowed, queries, keys_values, keys_values, carried)


def shards(
    db_tokens,
    db_parent,
    db_depth,
    nb_rows,
    seq_start,
    table,
    depth_table,
    enc_gain,
    enc_qkv,
    tree_bias,
    enc_wo,
    cond_kv,
    queries,
    cca_kv,
):
    seq_size = lax.axis_size("seq")
    tp_size = lax.axis_size("tp")
    block_count, pair_count = nb_rows.shape
    unit_count = block_count * pair_count
    stored, length = db_tokens.shape
    columns = table.shape[1]
    width = columns * tp_size
    rows_here = enc_qkv.shape[0]

    share = jnp.concatenate(
        [
            enc_qkv.transpose(1, 0, 2).reshape(3 * rows_here, columns),
            enc_wo.T,
            cca_kv.reshape(rows_here, columns),
        ],
        axis=0,
    )
    shares = lax.all_gather(share, ("seq", "tp"), axis=0).reshape(
        seq_size, tp_size, 5 * rows_here, columns
    )
    kv_cols = cca_kv.shape[2]

    cond_len = cond_kv.shape[0] // block_count
    my_blocks = block_count // tp_size
    cond = exchange(
        cond_kv.reshape(tp_size, my_blocks * cond_len, 2 * columns), "tp"
    )

    flat_rows = nb_rows.reshape(unit_count)
    holder = flat_rows // stored
    local_row = flat_rows % stored
    places = jnp.arange(seq_size, dtype=jnp.int32)
    request = jnp.sum(
        jnp.where(holder[None, :] == places[:, None], local_row[None, :], 0), axis=1
    )
    request = jnp.broadcast_to(request[:, None], (seq_size, 16))
    wanted = exchange(request, "seq")[:, 0]
    reply = jnp.concatenate(
        [
            jnp.take(db_tokens, wanted, axis=0),
            jnp.take(db_depth, wanted, axis=0),
            jnp.take(db_parent, wanted, axis=0),
        ],
        axis=1,
    )
    fetched = jnp.take(exchange(reply, "seq"), holder, axis=0)
    tokens = fetched[:, :length].reshape(unit_count * length)
    depths = fetched[:, length : 2 * length].reshape(unit_count * length)
    parents = fetched[:, 2 * length :]
    depth_hit = (
        depths[:, None] == jnp.arange(depth_table.shape[0], dtype=jnp.int32)[None, :]
    ).astype(jnp.bfloat16)
    embedded = (
        jnp.take(table, tokens, axis=0).astype(jnp.float32)
        + jnp.dot(depth_hit, depth_table, preferred_element_type=jnp.float32)
    ).astype(jnp.bfloat16)

    my_units = unit_count // tp_size
    pieces = exchange(embedded.reshape(tp_size, my_units * length, columns), "tp")
    parents = lax.dynamic_slice_in_dim(parents, lax.axis_index("tp") * my_units, my_units)
    parent_hit = (
        parents.reshape(my_units * length)[:, None] == jnp.arange(length, dtype=parents.dtype)[None, :]
    ).astype(jnp.bfloat16)
    place = jnp.arange(seq_size, dtype=jnp.int32)[None]
    outgoing = encoder(
        place,
        jnp.arange(tp_size, dtype=jnp.int32),
        tree_bias,
        pieces,
        enc_gain[None],
        parent_hit,
        cond,
        [("a", shares, 3 * SHARE, 0), ("o", shares, SHARE, 3), ("c", shares, SHARE, 4)],
        1,
        my_units,
        length,
        cond_len,
    )
    key_rows = pair_count * length
    keys_values = exchange(outgoing, "tp").reshape(unit_count * length, 2 * kv_cols)
    carried = lax.ppermute(
        keys_values[(block_count - 1) * key_rows :], "seq", [(s, s + 1) for s in range(seq_size - 1)]
    )
    block_index = lax.axis_index("seq") * block_count + jnp.arange(block_count, dtype=jnp.int32)
    allowed = (block_index > 0) & (seq_start == 0)
    return attend(allowed.astype(jnp.int32), queries, keys_values, carried, key_rows)


def solution(mesh):
    in_specs = (
        P("seq", None),
        P("seq", None),
        P("seq", None),
        P("seq", None),
        P("seq"),
        P(None, "tp"),
        P(None, "tp"),
        P(),
        P("seq", None, "tp"),
        P(),
        P("tp", "seq"),
        P("seq", None, "tp"),
        P("seq", "tp"),
        P("seq", None, "tp"),
    )
    out_specs = P("seq", "tp")
    return jax.shard_map(shards, mesh=mesh, in_specs=in_specs, out_specs=out_specs, check_vma=False)
```

```python
import functools
import math

import jax
import jax.numpy as jnp
from jax import lax
from jax.experimental import pallas as pl
from jax.experimental.pallas import tpu as pltpu
from jax.sharding import Mesh, PartitionSpec as P

HD = 128
SHARE = 16
SCALE = 1.0 / math.sqrt(HD)


SEQ = ("z", "y", "core")
SHIFTS = (0, 1, 3, 2)
FLIPS = (0, 4, 2, 6, 1, 5, 3, 7)


def exchange(value, axis):
    return lax.all_to_all(value, axis, split_axis=0, concat_axis=0, tiled=True)


def moved(value, axis, steps):
    count = lax.axis_size(axis)
    return lax.ppermute(value, axis, [(i, (i + steps) % count) for i in range(count)])


def swapped(value, axis, distance):
    count = lax.axis_size(axis)
    return lax.ppermute(value, axis, [(i, i ^ distance) for i in range(count)])


def doubled(value, axis, distance):
    return jnp.concatenate([value, swapped(value, axis, distance)], axis=0)


def ring(value, axis):
    return [value] + [moved(value, axis, d) for d in SHIFTS[1:]]


def assemble(refs, place_ref, target, first, count):
    for r, ref in enumerate(refs):
        slots = ref.shape[0]

        def copy(slot, carry, ref=ref, r=r):
            row = pl.multiple_of(place_ref[r, slot] * SHARE, SHARE)
            for a in range(count):
                target[first + a, pl.ds(row, SHARE), :] = ref[slot, pl.ds(a * SHARE, SHARE), :]
            return carry

        lax.fori_loop(0, slots, copy, 0, unroll=8)


def encoder_body(
    parts, my_units, length, cond_len, place_ref, xs_ref, bias_ref, emb_ref, gain_ref, hit_ref, cond_ref, *refs
):
    wa_refs, wo_refs, wc_refs = refs[:parts], refs[parts : 2 * parts], refs[2 * parts : 3 * parts]
    out_ref, normed_ref, acc_ref, enc_ref, mixed_ref, buf_ref = refs[3 * parts :]
    step = pl.program_id(0)
    pieces, rows, columns = emb_ref.shape
    width = pieces * columns
    nt = (((1,), (1,)), ((), ()))
    nn = (((1,), (0,)), ((), ()))

    @pl.when(step == 0)
    def _():
        for n in range(my_units):
            here = pl.ds(n * length, length)
            value = jnp.concatenate(
                [emb_ref[t, here, :].astype(jnp.float32) for t in range(pieces)], axis=1
            )
            acc_ref[here, :] = value
            mean = jnp.sum(value * value, axis=1, keepdims=True) * (1.0 / width)
            normed_ref[here, :] = (value * lax.rsqrt(mean + 1e-05) * gain_ref[...]).astype(jnp.bfloat16)

    @pl.when(step < pieces)
    def _():
        head = xs_ref[step] * (columns // HD)
        assemble(wa_refs, place_ref, buf_ref, 0, 3)
        assemble(wo_refs, place_ref, buf_ref, 3, 1)
        normed = normed_ref[...]
        project = lambda a: lax.dot_general(
            normed, buf_ref[a], nn, preferred_element_type=jnp.float32
        ).astype(jnp.bfloat16)
        query, key, value = project(0), project(1), project(2)
        for h in range(columns // HD):
            cols = slice(h * HD, (h + 1) * HD)
            bias = bias_ref[head + h]
            for n in range(my_units):
                here = slice(n * length, (n + 1) * length)
                block = n * length // (rows // (cond_ref.shape[1] // cond_len))
                cond_rows = pl.ds(block * cond_len, cond_len)
                q = query[here, cols]
                self_scores = lax.dot_general(
                    q, key[here, cols], nt, preferred_element_type=jnp.float32
                ) * SCALE + bias * hit_ref[here, :].astype(jnp.float32)
                cond_scores = (
                    lax.dot_general(
                        q,
                        cond_ref[0, cond_rows, pl.ds(h * HD, HD)],
                        nt,
                        preferred_element_type=jnp.float32,
                    )
                    * SCALE
                )
                top = jnp.maximum(
                    jnp.max(self_scores, axis=1, keepdims=True),
                    jnp.max(cond_scores, axis=1, keepdims=True),
                )
                self_e = jnp.exp(self_scores - top)
                cond_e = jnp.exp(cond_scores - top)
                inverse = 1.0 / (
                    jnp.sum(self_e, axis=1, keepdims=True) + jnp.sum(cond_e, axis=1, keepdims=True)
                )
                mixed = lax.dot_general(
                    (self_e * inverse).astype(jnp.bfloat16),
                    value[here, cols],
                    nn,
                    preferred_element_type=jnp.float32,
                ) + lax.dot_general(
                    (cond_e * inverse).astype(jnp.bfloat16),
                    cond_ref[0, cond_rows, pl.ds(columns + h * HD, HD)],
                    nn,
                    preferred_element_type=jnp.float32,
                )
                mixed_ref[here, cols] = mixed.astype(jnp.bfloat16)
        acc_ref[...] += lax.dot_general(
            mixed_ref[...], buf_ref[3], nt, preferred_element_type=jnp.float32
        )

    @pl.when(step == pieces)
    def _():
        enc_ref[...] = acc_ref[...].astype(jnp.bfloat16)

    @pl.when(step >= pieces)
    def _():
        assemble(wc_refs, place_ref, buf_ref, 4, 1)
        out_ref[0] = lax.dot_general(
            enc_ref[...], buf_ref[4], nn, preferred_element_type=jnp.float32
        ).astype(jnp.bfloat16)


def encoder(place, xs, bias, emb, gain, hit, cond, weights, my_units, length, cond_len):
    pieces, rows, columns = emb.shape
    width = pieces * columns
    last = pieces - 1
    full = lambda shape: pl.BlockSpec(shape, lambda i, p, x: (0,) * len(shape))
    specs = {"a": [], "o": [], "c": []}
    arrays = {"a": [], "o": [], "c": []}
    for kind, array, height, index in weights:
        pick = (
            (lambda i: jnp.minimum(i, last)) if kind in "ao" else (lambda i: jnp.maximum(i - pieces, 0))
        )
        specs[kind].append(
            pl.BlockSpec(
                (None, array.shape[1], height, columns),
                lambda i, p, x, pick=pick, index=index: (pick(i), 0, index, 0),
            )
        )
        arrays[kind].append(array)
    parts = len(specs["a"])
    return pl.pallas_call(
        functools.partial(encoder_body, parts, my_units, length, cond_len),
        out_shape=jax.ShapeDtypeStruct((pieces, rows, columns), jnp.bfloat16),
        grid_spec=pltpu.PrefetchScalarGridSpec(
            num_scalar_prefetch=2,
            grid=(2 * pieces,),
            in_specs=[
                pl.BlockSpec(memory_space=pltpu.SMEM),
                full(emb.shape),
                full(gain.shape),
                full(hit.shape),
                pl.BlockSpec(
                    (1,) + cond.shape[1:], lambda i, p, x: (jnp.minimum(i, last), 0, 0)
                ),
                *specs["a"],
                *specs["o"],
                *specs["c"],
            ],
            out_specs=pl.BlockSpec(
                (1, rows, columns), lambda i, p, x: (x[jnp.maximum(i - pieces, 0)], 0, 0)
            ),
            scratch_shapes=[
                pltpu.VMEM((rows, width), jnp.bfloat16),
                pltpu.VMEM((rows, width), jnp.float32),
                pltpu.VMEM((rows, width), jnp.bfloat16),
                pltpu.VMEM((rows, columns), jnp.bfloat16),
                pltpu.VMEM((5, width, columns), jnp.bfloat16),
            ],
        ),
        compiler_params=pltpu.CompilerParams(
            dimension_semantics=("arbitrary",), vmem_limit_bytes=48 * 1024 * 1024
        ),
        name="encoder",
    )(place, xs, bias, emb, gain, hit, cond, *arrays["a"], *arrays["o"], *arrays["c"])


def attend_body(heads, allowed_ref, q_ref, cur_ref, prev_ref, carried_ref, out_ref):
    block = pl.program_id(0)
    nt = (((1,), (1,)), ((), ()))
    nn = (((1,), (0,)), ((), ()))
    tokens = q_ref.shape[0]
    previous = jnp.where(block == 0, carried_ref[...], prev_ref[...])

    def mix(query, kv):
        scores = (
            lax.dot_general(query, kv[:, :HD], nt, preferred_element_type=jnp.float32) * SCALE
        )
        e = jnp.exp(scores - jnp.max(scores, axis=1, keepdims=True))
        weights = (e * (1.0 / jnp.sum(e, axis=1, keepdims=True))).astype(jnp.bfloat16)
        return lax.dot_general(weights, kv[:, HD:], nn, preferred_element_type=jnp.float32)

    query = jnp.concatenate([q_ref[:, pl.ds(h * HD, HD)] for h in range(heads)], axis=0)
    leading = mix(query, previous)
    leading = jnp.where(allowed_ref[block] > 0, leading, jnp.zeros_like(leading))
    final = jnp.concatenate(
        [q_ref[tokens - 8 :, pl.ds(h * HD, HD)].astype(jnp.float32)[7:8] for h in range(heads)], axis=0
    ).astype(jnp.bfloat16)
    trailing = mix(final, cur_ref[...])
    row = lax.broadcasted_iota(jnp.int32, (tokens, HD), 0)
    for h in range(heads):
        out_ref[:, pl.ds(h * HD, HD)] = jnp.where(
            row == tokens - 1,
            jnp.broadcast_to(trailing[h : h + 1], (tokens, HD)),
            leading[h * tokens : (h + 1) * tokens],
        ).astype(jnp.bfloat16)


def attend(allowed, queries, keys_values, carried, key_rows):
    block_count = allowed.shape[0]
    tokens = queries.shape[0] // block_count
    heads = queries.shape[1] // HD
    return pl.pallas_call(
        functools.partial(attend_body, heads),
        out_shape=jax.ShapeDtypeStruct(queries.shape, jnp.bfloat16),
        grid=(block_count,),
        in_specs=[
            pl.BlockSpec(memory_space=pltpu.SMEM),
            pl.BlockSpec((tokens, queries.shape[1]), lambda c: (c, 0)),
            pl.BlockSpec((key_rows, 2 * HD), lambda c: (c, 0)),
            pl.BlockSpec((key_rows, 2 * HD), lambda c: (jnp.maximum(c - 1, 0), 0)),
            pl.BlockSpec((key_rows, 2 * HD), lambda c: (0, 0)),
        ],
        out_specs=pl.BlockSpec((tokens, queries.shape[1]), lambda c: (c, 0)),
        compiler_params=pltpu.CompilerParams(dimension_semantics=("arbitrary",)),
        name="attend",
    )(allowed, queries, keys_values, keys_values, carried)


def shards(
    db_tokens,
    db_parent,
    db_depth,
    nb_rows,
    seq_start,
    table,
    depth_table,
    enc_gain,
    enc_qkv,
    tree_bias,
    enc_wo,
    cond_kv,
    queries,
    cca_kv,
):
    seq_size = math.prod(lax.axis_size(axis) for axis in SEQ)
    tp_size = lax.axis_size("tp")
    here = lax.axis_index("tp")
    block_count, pair_count = nb_rows.shape
    unit_count = block_count * pair_count
    stored, length = db_tokens.shape
    columns = table.shape[1]
    rows_here = enc_qkv.shape[0]
    kv_cols = cca_kv.shape[2]
    cond_len = cond_kv.shape[0] // block_count
    my_units = unit_count // tp_size
    my_tokens = cond_kv.shape[0] // tp_size
    key_rows = pair_count * length

    flat_rows = nb_rows.reshape(unit_count)
    holder = flat_rows // stored
    local_row = flat_rows % stored
    places = jnp.arange(seq_size, dtype=jnp.int32)
    request = jnp.sum(
        jnp.where(holder[None, :] == places[:, None], local_row[None, :], 0), axis=1
    )
    request = jnp.broadcast_to(request[:, None], (seq_size, 16))
    wanted = exchange(request, SEQ)[:, 0]

    share = jnp.concatenate(
        [
            enc_qkv.transpose(1, 0, 2).reshape(3 * rows_here, columns),
            enc_wo.T,
            cca_kv.reshape(rows_here, columns),
        ],
        axis=0,
    )[None]
    share = doubled(share, "z", 4)
    share, wanted = lax.optimization_barrier((share, wanted))
    share = doubled(share, "z", 2)
    reply = jnp.concatenate(
        [
            jnp.take(db_tokens, wanted, axis=0),
            jnp.take(db_depth, wanted, axis=0),
            jnp.take(db_parent, wanted, axis=0),
        ],
        axis=1,
    )
    fetched = exchange(reply, SEQ)
    share = doubled(share, "z", 1)
    conditioning = cond_kv.reshape(tp_size, my_tokens, 2 * columns)
    cond = jnp.stack(
        [
            moved(
                lax.dynamic_index_in_dim(conditioning, (here + d) % tp_size, 0, keepdims=False),
                "tp",
                d,
            )
            if d
            else lax.dynamic_index_in_dim(conditioning, here, 0, keepdims=False)
            for d in SHIFTS
        ]
    )
    in_rows, out_rows, fetched, cond = lax.optimization_barrier(
        (share[:, : 3 * rows_here], share[:, 3 * rows_here :], fetched, cond)
    )
    in_rows = ring(in_rows, "y")
    out_rows = ring(out_rows, "tp")

    fetched = jnp.take(fetched, holder, axis=0)
    tokens = fetched[:, :length].reshape(unit_count * length)
    depths = fetched[:, length : 2 * length].reshape(unit_count * length)
    parents = fetched[:, 2 * length :]
    depth_hit = (
        depths[:, None] == jnp.arange(depth_table.shape[0], dtype=jnp.int32)[None, :]
    ).astype(jnp.bfloat16)
    embedded = (
        jnp.take(table, tokens, axis=0).astype(jnp.float32)
        + jnp.dot(depth_hit, depth_table, preferred_element_type=jnp.float32)
    ).astype(jnp.bfloat16)
    in_rows, out_rows, embedded = lax.optimization_barrier((in_rows, out_rows, embedded))

    in_rows = jnp.stack(ring(jnp.concatenate(in_rows), "tp"))
    out_rows = jnp.stack(ring(jnp.stack(out_rows), "y"), axis=1)
    out_rows = out_rows.reshape(in_rows.shape[:2] + out_rows.shape[-2:])
    pieces = exchange(embedded.reshape(tp_size, my_units * length, columns), "tp")
    in_rows, out_rows, pieces = lax.optimization_barrier((in_rows, out_rows, pieces))
    in_pair = (in_rows, swapped(in_rows, "core", 1))
    out_pair = (out_rows, swapped(out_rows, "core", 1))

    shifts = jnp.array(SHIFTS, jnp.int32)
    z_of = lax.axis_index("z") ^ jnp.array(FLIPS, jnp.int32)
    y_of = (lax.axis_index("y") - shifts) % len(SHIFTS)
    core_of = lax.axis_index("core") ^ jnp.arange(2, dtype=jnp.int32)
    place = (
        (z_of[None, None, :] * len(SHIFTS) + y_of[None, :, None]) * 2 + core_of[:, None, None]
    ).reshape(2, -1)
    parents = lax.dynamic_slice_in_dim(parents, here * my_units, my_units)
    parent_hit = (
        parents.reshape(my_units * length)[:, None] == jnp.arange(length, dtype=parents.dtype)[None, :]
    ).astype(jnp.bfloat16)
    outgoing = encoder(
        place,
        (here - shifts) % tp_size,
        tree_bias,
        pieces,
        enc_gain[None],
        parent_hit,
        cond,
        [("a", rows, 3 * SHARE, 0) for rows in in_pair]
        + [("o", rows, SHARE, 0) for rows in out_pair]
        + [("c", rows, SHARE, 1) for rows in out_pair],
        my_units,
        length,
        cond_len,
    )
    keys_values = exchange(outgoing, "tp").reshape(unit_count * length, 2 * kv_cols)
    carried = lax.ppermute(
        keys_values[(block_count - 1) * key_rows :], SEQ, [(s, s + 1) for s in range(seq_size - 1)]
    )
    block_index = lax.axis_index(SEQ) * block_count + jnp.arange(block_count, dtype=jnp.int32)
    allowed = (block_index > 0) & (seq_start == 0)
    return attend(allowed.astype(jnp.int32), queries, keys_values, carried, key_rows)


def solution(mesh):
    split = Mesh(
        mesh.devices.reshape(8, 4, 2, mesh.shape["tp"]),
        SEQ + ("tp",),
    )
    in_specs = (
        P(SEQ, None),
        P(SEQ, None),
        P(SEQ, None),
        P(SEQ, None),
        P(SEQ),
        P(None, "tp"),
        P(None, "tp"),
        P(),
        P(SEQ, None, "tp"),
        P(),
        P("tp", SEQ),
        P(SEQ, None, "tp"),
        P(SEQ, "tp"),
        P(SEQ, None, "tp"),
    )
    out_specs = P(SEQ, "tp")
    return jax.shard_map(shards, mesh=split, in_specs=in_specs, out_specs=out_specs, check_vma=False)
```

```python
import functools
import math

import jax
import jax.numpy as jnp
from jax import lax
from jax.experimental import pallas as pl
from jax.experimental.pallas import tpu as pltpu
from jax.sharding import Mesh, PartitionSpec as P

HD = 128
SHARE = 16
SCALE = 1.0 / math.sqrt(HD)


SEQ = ("z", "y", "core")


def exchange(value, axis):
    return lax.all_to_all(value, axis, split_axis=0, concat_axis=0, tiled=True)


def swapped(value, axis, distance):
    count = lax.axis_size(axis)
    return lax.ppermute(value, axis, [(i, i ^ distance) for i in range(count)])


def doubled(value, axis, distance):
    return jnp.concatenate([value, swapped(value, axis, distance)], axis=0)


def assemble(refs, place_ref, target, first, count):
    for r, ref in enumerate(refs):
        slots = ref.shape[0]

        def copy(slot, carry, ref=ref, r=r):
            row = pl.multiple_of(place_ref[r, slot] * SHARE, SHARE)
            for a in range(count):
                target[first + a, pl.ds(row, SHARE), :] = ref[slot, pl.ds(a * SHARE, SHARE), :]
            return carry

        lax.fori_loop(0, slots, copy, 0, unroll=8)


def encoder_body(
    parts, my_units, length, cond_len, place_ref, xs_ref, bias_ref, emb_ref, gain_ref, hit_ref, cond_ref, *refs
):
    wa_refs, wo_refs, wc_refs = refs[:parts], refs[parts : 2 * parts], refs[2 * parts : 3 * parts]
    out_ref, normed_ref, acc_ref, enc_ref, mixed_ref, buf_ref = refs[3 * parts :]
    step = pl.program_id(0)
    pieces, rows, columns = emb_ref.shape
    width = pieces * columns
    nt = (((1,), (1,)), ((), ()))
    nn = (((1,), (0,)), ((), ()))

    @pl.when(step == 0)
    def _():
        for n in range(my_units):
            here = pl.ds(n * length, length)
            value = jnp.concatenate(
                [emb_ref[t, here, :].astype(jnp.float32) for t in range(pieces)], axis=1
            )
            acc_ref[here, :] = value
            mean = jnp.sum(value * value, axis=1, keepdims=True) * (1.0 / width)
            normed_ref[here, :] = (value * lax.rsqrt(mean + 1e-05) * gain_ref[...]).astype(jnp.bfloat16)

    @pl.when(step < pieces)
    def _():
        head = xs_ref[step] * (columns // HD)
        assemble(wa_refs, place_ref, buf_ref, 0, 3)
        assemble(wo_refs, place_ref, buf_ref, 3, 1)
        normed = normed_ref[...]
        project = lambda a: lax.dot_general(
            normed, buf_ref[a], nn, preferred_element_type=jnp.float32
        ).astype(jnp.bfloat16)
        query, key, value = project(0), project(1), project(2)
        for h in range(columns // HD):
            cols = slice(h * HD, (h + 1) * HD)
            bias = bias_ref[head + h]
            for n in range(my_units):
                here = slice(n * length, (n + 1) * length)
                block = n * length // (rows // (cond_ref.shape[1] // cond_len))
                cond_rows = pl.ds(block * cond_len, cond_len)
                q = query[here, cols]
                self_scores = lax.dot_general(
                    q, key[here, cols], nt, preferred_element_type=jnp.float32
                ) * SCALE + bias * hit_ref[here, :].astype(jnp.float32)
                cond_scores = (
                    lax.dot_general(
                        q,
                        cond_ref[0, cond_rows, pl.ds(h * HD, HD)],
                        nt,
                        preferred_element_type=jnp.float32,
                    )
                    * SCALE
                )
                top = jnp.maximum(
                    jnp.max(self_scores, axis=1, keepdims=True),
                    jnp.max(cond_scores, axis=1, keepdims=True),
                )
                self_e = jnp.exp(self_scores - top)
                cond_e = jnp.exp(cond_scores - top)
                inverse = 1.0 / (
                    jnp.sum(self_e, axis=1, keepdims=True) + jnp.sum(cond_e, axis=1, keepdims=True)
                )
                mixed = lax.dot_general(
                    (self_e * inverse).astype(jnp.bfloat16),
                    value[here, cols],
                    nn,
                    preferred_element_type=jnp.float32,
                ) + lax.dot_general(
                    (cond_e * inverse).astype(jnp.bfloat16),
                    cond_ref[0, cond_rows, pl.ds(columns + h * HD, HD)],
                    nn,
                    preferred_element_type=jnp.float32,
                )
                mixed_ref[here, cols] = mixed.astype(jnp.bfloat16)
        acc_ref[...] += lax.dot_general(
            mixed_ref[...], buf_ref[3], nt, preferred_element_type=jnp.float32
        )

    @pl.when(step == pieces)
    def _():
        enc_ref[...] = acc_ref[...].astype(jnp.bfloat16)

    @pl.when(step >= pieces)
    def _():
        assemble(wc_refs, place_ref, buf_ref, 4, 1)
        out_ref[0] = lax.dot_general(
            enc_ref[...], buf_ref[4], nn, preferred_element_type=jnp.float32
        ).astype(jnp.bfloat16)


def encoder(place, xs, bias, emb, gain, hit, cond, weights, my_units, length, cond_len):
    pieces, rows, columns = emb.shape
    width = pieces * columns
    last = pieces - 1
    full = lambda shape: pl.BlockSpec(shape, lambda i, p, x: (0,) * len(shape))
    specs = {"a": [], "o": [], "c": []}
    arrays = {"a": [], "o": [], "c": []}
    for kind, array, height, index in weights:
        pick = (
            (lambda i: jnp.minimum(i, last)) if kind in "ao" else (lambda i: jnp.maximum(i - pieces, 0))
        )
        specs[kind].append(
            pl.BlockSpec(
                (None, array.shape[1], height, columns),
                lambda i, p, x, pick=pick, index=index: (pick(i), 0, index, 0),
            )
        )
        arrays[kind].append(array)
    parts = len(specs["a"])
    return pl.pallas_call(
        functools.partial(encoder_body, parts, my_units, length, cond_len),
        out_shape=jax.ShapeDtypeStruct((pieces, rows, columns), jnp.bfloat16),
        grid_spec=pltpu.PrefetchScalarGridSpec(
            num_scalar_prefetch=2,
            grid=(2 * pieces,),
            in_specs=[
                pl.BlockSpec(memory_space=pltpu.SMEM),
                full(emb.shape),
                full(gain.shape),
                full(hit.shape),
                pl.BlockSpec(
                    (1,) + cond.shape[1:], lambda i, p, x: (jnp.minimum(i, last), 0, 0)
                ),
                *specs["a"],
                *specs["o"],
                *specs["c"],
            ],
            out_specs=pl.BlockSpec(
                (1, rows, columns), lambda i, p, x: (x[jnp.maximum(i - pieces, 0)], 0, 0)
            ),
            scratch_shapes=[
                pltpu.VMEM((rows, width), jnp.bfloat16),
                pltpu.VMEM((rows, width), jnp.float32),
                pltpu.VMEM((rows, width), jnp.bfloat16),
                pltpu.VMEM((rows, columns), jnp.bfloat16),
                pltpu.VMEM((5, width, columns), jnp.bfloat16),
            ],
        ),
        compiler_params=pltpu.CompilerParams(
            dimension_semantics=("arbitrary",), vmem_limit_bytes=48 * 1024 * 1024
        ),
        name="encoder",
    )(place, xs, bias, emb, gain, hit, cond, *arrays["a"], *arrays["o"], *arrays["c"])


def attend_body(heads, allowed_ref, q_ref, cur_ref, prev_ref, carried_ref, out_ref):
    block = pl.program_id(0)
    nt = (((1,), (1,)), ((), ()))
    nn = (((1,), (0,)), ((), ()))
    tokens = q_ref.shape[0]
    previous = jnp.where(block == 0, carried_ref[...], prev_ref[...])

    def mix(query, kv):
        scores = (
            lax.dot_general(query, kv[:, :HD], nt, preferred_element_type=jnp.float32) * SCALE
        )
        e = jnp.exp(scores - jnp.max(scores, axis=1, keepdims=True))
        weights = (e * (1.0 / jnp.sum(e, axis=1, keepdims=True))).astype(jnp.bfloat16)
        return lax.dot_general(weights, kv[:, HD:], nn, preferred_element_type=jnp.float32)

    query = jnp.concatenate([q_ref[:, pl.ds(h * HD, HD)] for h in range(heads)], axis=0)
    leading = mix(query, previous)
    leading = jnp.where(allowed_ref[block] > 0, leading, jnp.zeros_like(leading))
    final = jnp.concatenate(
        [q_ref[tokens - 8 :, pl.ds(h * HD, HD)].astype(jnp.float32)[7:8] for h in range(heads)], axis=0
    ).astype(jnp.bfloat16)
    trailing = mix(final, cur_ref[...])
    row = lax.broadcasted_iota(jnp.int32, (tokens, HD), 0)
    for h in range(heads):
        out_ref[:, pl.ds(h * HD, HD)] = jnp.where(
            row == tokens - 1,
            jnp.broadcast_to(trailing[h : h + 1], (tokens, HD)),
            leading[h * tokens : (h + 1) * tokens],
        ).astype(jnp.bfloat16)


def attend(allowed, queries, keys_values, carried, key_rows):
    block_count = allowed.shape[0]
    tokens = queries.shape[0] // block_count
    heads = queries.shape[1] // HD
    return pl.pallas_call(
        functools.partial(attend_body, heads),
        out_shape=jax.ShapeDtypeStruct(queries.shape, jnp.bfloat16),
        grid=(block_count,),
        in_specs=[
            pl.BlockSpec(memory_space=pltpu.SMEM),
            pl.BlockSpec((tokens, queries.shape[1]), lambda c: (c, 0)),
            pl.BlockSpec((key_rows, 2 * HD), lambda c: (c, 0)),
            pl.BlockSpec((key_rows, 2 * HD), lambda c: (jnp.maximum(c - 1, 0), 0)),
            pl.BlockSpec((key_rows, 2 * HD), lambda c: (0, 0)),
        ],
        out_specs=pl.BlockSpec((tokens, queries.shape[1]), lambda c: (c, 0)),
        compiler_params=pltpu.CompilerParams(dimension_semantics=("arbitrary",)),
        name="attend",
    )(allowed, queries, keys_values, keys_values, carried)


def shards(
    db_tokens,
    db_parent,
    db_depth,
    nb_rows,
    seq_start,
    table,
    depth_table,
    enc_gain,
    enc_qkv,
    tree_bias,
    enc_wo,
    cond_kv,
    queries,
    cca_kv,
):
    seq_size = math.prod(lax.axis_size(axis) for axis in SEQ)
    tp_size = lax.axis_size("tp")
    here = lax.axis_index("tp")
    block_count, pair_count = nb_rows.shape
    unit_count = block_count * pair_count
    stored, length = db_tokens.shape
    columns = table.shape[1]
    rows_here = enc_qkv.shape[0]
    kv_cols = cca_kv.shape[2]
    cond_len = cond_kv.shape[0] // block_count
    my_units = unit_count // tp_size
    my_tokens = cond_kv.shape[0] // tp_size
    key_rows = pair_count * length

    flat_rows = nb_rows.reshape(unit_count)
    holder = flat_rows // stored
    local_row = flat_rows % stored
    places = jnp.arange(seq_size, dtype=jnp.int32)
    request = jnp.sum(
        jnp.where(holder[None, :] == places[:, None], local_row[None, :], 0), axis=1
    )
    request = jnp.broadcast_to(request[:, None], (seq_size, 16))

    share = jnp.concatenate(
        [
            enc_qkv.transpose(1, 0, 2).reshape(3 * rows_here, columns),
            enc_wo.T,
            cca_kv.reshape(rows_here, columns),
        ],
        axis=0,
    )[None]
    share = doubled(share, "z", 4)
    share, request = lax.optimization_barrier((share, request))
    share = doubled(share, "z", 2)
    wanted = exchange(request, SEQ)[:, 0]
    share, wanted = lax.optimization_barrier((share, wanted))
    share = doubled(share, "z", 1)
    reply = jnp.concatenate(
        [
            jnp.take(db_tokens, wanted, axis=0),
            jnp.take(db_depth, wanted, axis=0),
            jnp.take(db_parent, wanted, axis=0),
        ],
        axis=1,
    )
    fetched = exchange(reply, SEQ)
    z_count = lax.axis_size("z")
    shares = lax.all_gather(
        share.reshape(z_count * 5 * rows_here, columns), ("tp", "y", "core"), axis=0
    ).reshape(tp_size, seq_size, 5 * rows_here, columns)
    cond = exchange(cond_kv.reshape(tp_size, my_tokens, 2 * columns), "tp")

    fetched = jnp.take(fetched, holder, axis=0)
    tokens = fetched[:, :length].reshape(unit_count * length)
    depths = fetched[:, length : 2 * length].reshape(unit_count * length)
    parents = fetched[:, 2 * length :]
    depth_hit = (
        depths[:, None] == jnp.arange(depth_table.shape[0], dtype=jnp.int32)[None, :]
    ).astype(jnp.bfloat16)
    embedded = (
        jnp.take(table, tokens, axis=0).astype(jnp.float32)
        + jnp.dot(depth_hit, depth_table, preferred_element_type=jnp.float32)
    ).astype(jnp.bfloat16)
    pieces = exchange(embedded.reshape(tp_size, my_units * length, columns), "tp")
    slot = jnp.arange(seq_size, dtype=jnp.int32)
    flip = slot % z_count
    flip = 4 * (flip & 1) + (flip & 2) + flip // 4
    place = ((lax.axis_index("z") ^ flip) * (seq_size // z_count) + slot // z_count)[None]
    parents = lax.dynamic_slice_in_dim(parents, here * my_units, my_units)
    parent_hit = (
        parents.reshape(my_units * length)[:, None] == jnp.arange(length, dtype=parents.dtype)[None, :]
    ).astype(jnp.bfloat16)
    outgoing = encoder(
        place,
        jnp.arange(tp_size, dtype=jnp.int32),
        tree_bias,
        pieces,
        enc_gain[None],
        parent_hit,
        cond,
        [("a", shares, 3 * SHARE, 0), ("o", shares, SHARE, 3), ("c", shares, SHARE, 4)],
        my_units,
        length,
        cond_len,
    )
    keys_values = exchange(outgoing, "tp").reshape(unit_count * length, 2 * kv_cols)
    carried = lax.ppermute(
        keys_values[(block_count - 1) * key_rows :], SEQ, [(s, s + 1) for s in range(seq_size - 1)]
    )
    block_index = lax.axis_index(SEQ) * block_count + jnp.arange(block_count, dtype=jnp.int32)
    allowed = (block_index > 0) & (seq_start == 0)
    return attend(allowed.astype(jnp.int32), queries, keys_values, carried, key_rows)


def solution(mesh):
    split = Mesh(
        mesh.devices.reshape(8, 4, 2, mesh.shape["tp"]),
        SEQ + ("tp",),
    )
    in_specs = (
        P(SEQ, None),
        P(SEQ, None),
        P(SEQ, None),
        P(SEQ, None),
        P(SEQ),
        P(None, "tp"),
        P(None, "tp"),
        P(),
        P(SEQ, None, "tp"),
        P(),
        P("tp", SEQ),
        P(SEQ, None, "tp"),
        P(SEQ, "tp"),
        P(SEQ, None, "tp"),
    )
    out_specs = P(SEQ, "tp")
    return jax.shard_map(shards, mesh=split, in_specs=in_specs, out_specs=out_specs, check_vma=False)
```

```python
import functools
import math

import jax
import jax.numpy as jnp
from jax import lax
from jax.experimental import pallas as pl
from jax.experimental.pallas import tpu as pltpu
from jax.sharding import Mesh, PartitionSpec as P

HD = 128
SHARE = 16
GROUP = 4
SCALE = 1.0 / math.sqrt(HD)


SEQ = ("z", "y", "core")


def exchange(value, axis):
    return lax.all_to_all(value, axis, split_axis=0, concat_axis=0, tiled=True)


def swapped(value, axis, distance):
    count = lax.axis_size(axis)
    return lax.ppermute(value, axis, [(i, i ^ distance) for i in range(count)])


def doubled(value, axis, distance):
    return jnp.concatenate([value, swapped(value, axis, distance)], axis=0)


def assemble(refs, place_ref, target, first, count):
    for r, ref in enumerate(refs):
        slots = ref.shape[0]

        def copy(slot, carry, ref=ref, r=r):
            row = pl.multiple_of(place_ref[r, slot] * SHARE, SHARE)
            for a in range(count):
                target[first + a, pl.ds(row, SHARE), :] = ref[slot, pl.ds(a * SHARE, SHARE), :]
            return carry

        lax.fori_loop(0, slots, copy, 0, unroll=8)


def encoder_body(
    parts, my_units, length, cond_len, place_ref, xs_ref, bias_ref, emb_ref, gain_ref, hit_ref, cond_ref, *refs
):
    wa_refs, wo_refs, wc_refs = refs[:parts], refs[parts : 2 * parts], refs[2 * parts : 3 * parts]
    out_ref, normed_ref, acc_ref, enc_ref, mixed_ref, buf_ref = refs[3 * parts :]
    step = pl.program_id(0)
    pieces, rows, columns = emb_ref.shape
    width = pieces * columns
    nt = (((1,), (1,)), ((), ()))
    nn = (((1,), (0,)), ((), ()))

    @pl.when(step == 0)
    def _():
        for n in range(my_units):
            here = pl.ds(n * length, length)
            value = jnp.concatenate(
                [emb_ref[t, here, :].astype(jnp.float32) for t in range(pieces)], axis=1
            )
            acc_ref[here, :] = value
            mean = jnp.sum(value * value, axis=1, keepdims=True) * (1.0 / width)
            normed_ref[here, :] = (value * lax.rsqrt(mean + 1e-05) * gain_ref[...]).astype(jnp.bfloat16)

    @pl.when(step < pieces)
    def _():
        head = xs_ref[step] * (columns // HD)
        assemble(wa_refs, place_ref, buf_ref, 0, 3)
        assemble(wo_refs, place_ref, buf_ref, 3, 1)
        normed = normed_ref[...]
        project = lambda a: lax.dot_general(
            normed, buf_ref[a], nn, preferred_element_type=jnp.float32
        ).astype(jnp.bfloat16)
        query, key, value = project(0), project(1), project(2)
        hit = hit_ref[...].astype(jnp.float32)
        per_block = rows // (cond_ref.shape[1] // cond_len)
        for h in range(columns // HD):
            cols = slice(h * HD, (h + 1) * HD)
            scores, mixing = [], []
            for n in range(my_units):
                here = slice(n * length, (n + 1) * length)
                cond_rows = pl.ds(n * length // per_block * cond_len, cond_len)
                cond_key = cond_ref[0, cond_rows, pl.ds(h * HD, HD)]
                cond_value = cond_ref[0, cond_rows, pl.ds(columns + h * HD, HD)]
                keys = jnp.concatenate([key[here, cols], cond_key, cond_key], axis=0)
                mixing.append(jnp.concatenate([value[here, cols], cond_value, cond_value], axis=0))
                scores.append(
                    lax.dot_general(query[here, cols], keys, nt, preferred_element_type=jnp.float32)
                )
            scores = jnp.concatenate(scores, axis=0) * SCALE
            self_scores = scores[:, :length] + bias_ref[head + h] * hit
            cond_scores = scores[:, length:]
            top = jnp.max(jnp.maximum(self_scores, cond_scores), axis=1, keepdims=True)
            self_e = jnp.exp(self_scores - top)
            cond_e = 0.5 * jnp.exp(cond_scores - top)
            inverse = 1.0 / jnp.sum(self_e + cond_e, axis=1, keepdims=True)
            weights = jnp.concatenate([self_e * inverse, cond_e * inverse], axis=1).astype(jnp.bfloat16)
            for n in range(my_units):
                here = slice(n * length, (n + 1) * length)
                mixed_ref[here, cols] = lax.dot_general(
                    weights[here], mixing[n], nn, preferred_element_type=jnp.float32
                ).astype(jnp.bfloat16)
        acc_ref[...] += lax.dot_general(
            mixed_ref[...], buf_ref[3], nt, preferred_element_type=jnp.float32
        )

    @pl.when(step == pieces)
    def _():
        enc_ref[...] = acc_ref[...].astype(jnp.bfloat16)

    @pl.when(step >= pieces)
    def _():
        assemble(wc_refs, place_ref, buf_ref, 4, 1)
        out_ref[0] = lax.dot_general(
            enc_ref[...], buf_ref[4], nn, preferred_element_type=jnp.float32
        ).astype(jnp.bfloat16)


def encoder(place, xs, bias, emb, gain, hit, cond, weights, my_units, length, cond_len):
    pieces, rows, columns = emb.shape
    width = pieces * columns
    last = pieces - 1
    full = lambda shape: pl.BlockSpec(shape, lambda i, p, x: (0,) * len(shape))
    specs = {"a": [], "o": [], "c": []}
    arrays = {"a": [], "o": [], "c": []}
    for kind, array, height, index in weights:
        pick = (
            (lambda i: jnp.minimum(i, last)) if kind in "ao" else (lambda i: jnp.maximum(i - pieces, 0))
        )
        specs[kind].append(
            pl.BlockSpec(
                (None, array.shape[1], height, columns),
                lambda i, p, x, pick=pick, index=index: (pick(i), 0, index, 0),
            )
        )
        arrays[kind].append(array)
    parts = len(specs["a"])
    return pl.pallas_call(
        functools.partial(encoder_body, parts, my_units, length, cond_len),
        out_shape=jax.ShapeDtypeStruct((pieces, rows, columns), jnp.bfloat16),
        grid_spec=pltpu.PrefetchScalarGridSpec(
            num_scalar_prefetch=2,
            grid=(2 * pieces,),
            in_specs=[
                pl.BlockSpec(memory_space=pltpu.SMEM),
                full(emb.shape),
                full(gain.shape),
                full(hit.shape),
                pl.BlockSpec(
                    (1,) + cond.shape[1:], lambda i, p, x: (jnp.minimum(i, last), 0, 0)
                ),
                *specs["a"],
                *specs["o"],
                *specs["c"],
            ],
            out_specs=pl.BlockSpec(
                (1, rows, columns), lambda i, p, x: (x[jnp.maximum(i - pieces, 0)], 0, 0)
            ),
            scratch_shapes=[
                pltpu.VMEM((rows, width), jnp.bfloat16),
                pltpu.VMEM((rows, width), jnp.float32),
                pltpu.VMEM((rows, width), jnp.bfloat16),
                pltpu.VMEM((rows, columns), jnp.bfloat16),
                pltpu.VMEM((5, width, columns), jnp.bfloat16),
            ],
        ),
        compiler_params=pltpu.CompilerParams(
            dimension_semantics=("arbitrary",), vmem_limit_bytes=48 * 1024 * 1024
        ),
        name="encoder",
    )(place, xs, bias, emb, gain, hit, cond, *arrays["a"], *arrays["o"], *arrays["c"])


def attend_body(heads, group, allowed_ref, q_ref, cur_ref, prev_ref, carried_ref, out_ref):
    step = pl.program_id(0)
    nt = (((1,), (1,)), ((), ()))
    nn = (((1,), (0,)), ((), ()))
    tokens = q_ref.shape[0] // group
    key_rows = cur_ref.shape[0] // group
    row = lax.broadcasted_iota(jnp.int32, (tokens, HD), 0)

    def mix(query, kv):
        scores = (
            lax.dot_general(query, kv[:, :HD], nt, preferred_element_type=jnp.float32) * SCALE
        )
        e = jnp.exp(scores - jnp.max(scores, axis=1, keepdims=True))
        weights = (e * (1.0 / jnp.sum(e, axis=1, keepdims=True))).astype(jnp.bfloat16)
        return lax.dot_general(weights, kv[:, HD:], nn, preferred_element_type=jnp.float32)

    for b in range(group):
        here = pl.ds(b * tokens, tokens)
        if b:
            previous = cur_ref[pl.ds((b - 1) * key_rows, key_rows), :]
        else:
            previous = jnp.where(step == 0, carried_ref[...], prev_ref[...])
        query = jnp.concatenate([q_ref[here, pl.ds(h * HD, HD)] for h in range(heads)], axis=0)
        leading = mix(query, previous)
        leading = jnp.where(
            allowed_ref[step * group + b] > 0, leading, jnp.zeros_like(leading)
        )
        tail = pl.ds((b + 1) * tokens - 8, 8)
        final = jnp.concatenate(
            [q_ref[tail, pl.ds(h * HD, HD)].astype(jnp.float32)[7:8] for h in range(heads)], axis=0
        ).astype(jnp.bfloat16)
        trailing = mix(final, cur_ref[pl.ds(b * key_rows, key_rows), :])
        for h in range(heads):
            out_ref[here, pl.ds(h * HD, HD)] = jnp.where(
                row == tokens - 1,
                jnp.broadcast_to(trailing[h : h + 1], (tokens, HD)),
                leading[h * tokens : (h + 1) * tokens],
            ).astype(jnp.bfloat16)


def attend(allowed, queries, keys_values, carried, key_rows):
    block_count = allowed.shape[0]
    group = GROUP
    tokens = queries.shape[0] // block_count
    heads = queries.shape[1] // HD
    return pl.pallas_call(
        functools.partial(attend_body, heads, group),
        out_shape=jax.ShapeDtypeStruct(queries.shape, jnp.bfloat16),
        grid=(block_count // group,),
        in_specs=[
            pl.BlockSpec(memory_space=pltpu.SMEM),
            pl.BlockSpec((group * tokens, queries.shape[1]), lambda c: (c, 0)),
            pl.BlockSpec((group * key_rows, 2 * HD), lambda c: (c, 0)),
            pl.BlockSpec((key_rows, 2 * HD), lambda c: (jnp.maximum(group * c - 1, 0), 0)),
            pl.BlockSpec((key_rows, 2 * HD), lambda c: (0, 0)),
        ],
        out_specs=pl.BlockSpec((group * tokens, queries.shape[1]), lambda c: (c, 0)),
        compiler_params=pltpu.CompilerParams(dimension_semantics=("arbitrary",)),
        name="attend",
    )(allowed, queries, keys_values, keys_values, carried)


def parts(
    db_tokens,
    db_parent,
    db_depth,
    nb_rows,
    seq_start,
    table,
    depth_table,
    enc_gain,
    enc_qkv,
    tree_bias,
    enc_wo,
    cond_kv,
    queries,
    cca_kv,
):
    seq_size = math.prod(lax.axis_size(axis) for axis in SEQ)
    tp_size = lax.axis_size("tp")
    here = lax.axis_index("tp")
    block_count, pair_count = nb_rows.shape
    unit_count = block_count * pair_count
    stored, length = db_tokens.shape
    columns = table.shape[1]
    rows_here = enc_qkv.shape[0]
    kv_cols = cca_kv.shape[2]
    cond_len = cond_kv.shape[0] // block_count
    my_units = unit_count // tp_size
    my_tokens = cond_kv.shape[0] // tp_size
    key_rows = pair_count * length

    flat_rows = nb_rows.reshape(unit_count)
    holder = flat_rows // stored
    local_row = flat_rows % stored
    places = jnp.arange(seq_size, dtype=jnp.int32)
    request = jnp.sum(
        jnp.where(holder[None, :] == places[:, None], local_row[None, :], 0), axis=1
    )
    request = jnp.broadcast_to(request[:, None], (seq_size, 16))

    share = jnp.concatenate(
        [
            enc_qkv.transpose(1, 0, 2).reshape(3 * rows_here, columns),
            enc_wo.T,
            cca_kv.reshape(rows_here, columns),
        ],
        axis=0,
    )[None]
    share = doubled(share, "z", 4)
    share = doubled(share, "z", 2)
    wanted = exchange(request, SEQ)[:, 0]
    share = doubled(share, "z", 1)
    reply = jnp.concatenate(
        [
            jnp.take(db_tokens, wanted, axis=0),
            jnp.take(db_depth, wanted, axis=0),
            jnp.take(db_parent, wanted, axis=0),
        ],
        axis=1,
    )
    fetched = exchange(reply, SEQ)
    z_count = lax.axis_size("z")
    shares = lax.all_gather(
        share.reshape(z_count * 5 * rows_here, columns), ("tp", "y", "core"), axis=0
    ).reshape(tp_size, seq_size, 5 * rows_here, columns)
    cond = exchange(cond_kv.reshape(tp_size, my_tokens, 2 * columns), "tp")

    fetched = jnp.take(fetched, holder, axis=0)
    tokens = fetched[:, :length].reshape(unit_count * length)
    depths = fetched[:, length : 2 * length].reshape(unit_count * length)
    parents = fetched[:, 2 * length :]
    depth_hit = (
        depths[:, None] == jnp.arange(depth_table.shape[0], dtype=jnp.int32)[None, :]
    ).astype(jnp.bfloat16)
    embedded = (
        jnp.take(table, tokens, axis=0).astype(jnp.float32)
        + jnp.dot(depth_hit, depth_table, preferred_element_type=jnp.float32)
    ).astype(jnp.bfloat16)
    pieces = exchange(embedded.reshape(tp_size, my_units * length, columns), "tp")
    slot = jnp.arange(seq_size, dtype=jnp.int32)
    flip = slot % z_count
    flip = 4 * (flip & 1) + (flip & 2) + flip // 4
    place = ((lax.axis_index("z") ^ flip) * (seq_size // z_count) + slot // z_count)[None]
    parents = lax.dynamic_slice_in_dim(parents, here * my_units, my_units)
    parent_hit = (
        parents.reshape(my_units * length)[:, None] == jnp.arange(length, dtype=parents.dtype)[None, :]
    ).astype(jnp.bfloat16)
    outgoing = encoder(
        place,
        jnp.arange(tp_size, dtype=jnp.int32),
        tree_bias,
        pieces,
        enc_gain[None],
        parent_hit,
        cond,
        [("a", shares, 3 * SHARE, 0), ("o", shares, SHARE, 3), ("c", shares, SHARE, 4)],
        my_units,
        length,
        cond_len,
    )
    keys_values = exchange(outgoing, "tp").reshape(unit_count * length, 2 * kv_cols)
    carried = lax.ppermute(
        keys_values[(block_count - 1) * key_rows :], SEQ, [(s, s + 1) for s in range(seq_size - 1)]
    )
    block_index = lax.axis_index(SEQ) * block_count + jnp.arange(block_count, dtype=jnp.int32)
    allowed = (block_index > 0) & (seq_start == 0)
    return attend(allowed.astype(jnp.int32), queries, keys_values, carried, key_rows)


def solution(mesh):
    split = Mesh(
        mesh.devices.reshape(8, 4, 2, mesh.shape["tp"]),
        SEQ + ("tp",),
    )
    in_specs = (
        P(SEQ, None),
        P(SEQ, None),
        P(SEQ, None),
        P(SEQ, None),
        P(SEQ),
        P(None, "tp"),
        P(None, "tp"),
        P(),
        P(SEQ, None, "tp"),
        P(),
        P("tp", SEQ),
        P(SEQ, None, "tp"),
        P(SEQ, "tp"),
        P(SEQ, None, "tp"),
    )
    out_specs = P(SEQ, "tp")
    return jax.shard_map(parts, mesh=split, in_specs=in_specs, out_specs=out_specs, check_vma=False)
```

```python
import functools
import math

import jax
import jax.numpy as jnp
from jax import lax
from jax.experimental import pallas as pl
from jax.experimental.pallas import tpu as pltpu
from jax.sharding import Mesh, PartitionSpec as P

HD = 128
SHARE = 16
GROUP = 4
SCALE = 1.0 / math.sqrt(HD)


SEQ = ("z", "y", "core")
TURNS = (0, 1, -1, 2)


def exchange(value, axis):
    return lax.all_to_all(value, axis, split_axis=0, concat_axis=0, tiled=True)


def moved(value, axis, steps):
    count = lax.axis_size(axis)
    return lax.ppermute(value, axis, [(i, (i + steps) % count) for i in range(count)])


def swapped(value, axis, distance):
    count = lax.axis_size(axis)
    return lax.ppermute(value, axis, [(i, i ^ distance) for i in range(count)])


def doubled(value, axis, distance):
    return jnp.concatenate([value, swapped(value, axis, distance)], axis=0)


def assemble(refs, place_ref, target, first, count):
    for r, ref in enumerate(refs):
        slots = ref.shape[0]

        def copy(slot, carry, ref=ref, r=r):
            row = pl.multiple_of(place_ref[r, slot] * SHARE, SHARE)
            for a in range(count):
                target[first + a, pl.ds(row, SHARE), :] = ref[slot, pl.ds(a * SHARE, SHARE), :]
            return carry

        lax.fori_loop(0, slots, copy, 0, unroll=8)


def encoder_body(
    parts, my_units, length, cond_len, place_ref, xs_ref, bias_ref, emb_ref, gain_ref, hit_ref, cond_ref, *refs
):
    wa_refs, wo_refs, wc_refs = refs[:parts], refs[parts : 2 * parts], refs[2 * parts : 3 * parts]
    out_ref, normed_ref, acc_ref, enc_ref, mixed_ref, buf_ref = refs[3 * parts :]
    step = pl.program_id(0)
    pieces, rows, columns = emb_ref.shape
    width = pieces * columns
    nt = (((1,), (1,)), ((), ()))
    nn = (((1,), (0,)), ((), ()))

    @pl.when(step == 0)
    def _():
        for n in range(my_units):
            here = pl.ds(n * length, length)
            value = jnp.concatenate(
                [emb_ref[t, here, :].astype(jnp.float32) for t in range(pieces)], axis=1
            )
            acc_ref[here, :] = value
            mean = jnp.sum(value * value, axis=1, keepdims=True) * (1.0 / width)
            normed_ref[here, :] = (value * lax.rsqrt(mean + 1e-05) * gain_ref[...]).astype(jnp.bfloat16)

    @pl.when(step < pieces)
    def _():
        head = step * (columns // HD)
        assemble(wa_refs, place_ref, buf_ref, 0, 3)
        assemble(wo_refs, place_ref, buf_ref, 3, 1)
        normed = normed_ref[...]
        project = lambda a: lax.dot_general(
            normed, buf_ref[a], nn, preferred_element_type=jnp.float32
        ).astype(jnp.bfloat16)
        query, key, value = project(0), project(1), project(2)
        hit = hit_ref[...].astype(jnp.float32)
        per_block = rows // (cond_ref.shape[1] // cond_len)
        for h in range(columns // HD):
            cols = slice(h * HD, (h + 1) * HD)
            scores, mixing = [], []
            for n in range(my_units):
                here = slice(n * length, (n + 1) * length)
                cond_rows = pl.ds(n * length // per_block * cond_len, cond_len)
                cond_key = cond_ref[0, cond_rows, pl.ds(h * HD, HD)]
                cond_value = cond_ref[0, cond_rows, pl.ds(columns + h * HD, HD)]
                keys = jnp.concatenate([key[here, cols], cond_key, cond_key], axis=0)
                mixing.append(jnp.concatenate([value[here, cols], cond_value, cond_value], axis=0))
                scores.append(
                    lax.dot_general(query[here, cols], keys, nt, preferred_element_type=jnp.float32)
                )
            scores = jnp.concatenate(scores, axis=0) * SCALE
            self_scores = scores[:, :length] + bias_ref[head + h] * hit
            cond_scores = scores[:, length:]
            top = jnp.max(jnp.maximum(self_scores, cond_scores), axis=1, keepdims=True)
            self_e = jnp.exp(self_scores - top)
            cond_e = 0.5 * jnp.exp(cond_scores - top)
            inverse = 1.0 / jnp.sum(self_e + cond_e, axis=1, keepdims=True)
            weights = jnp.concatenate([self_e * inverse, cond_e * inverse], axis=1).astype(jnp.bfloat16)
            for n in range(my_units):
                here = slice(n * length, (n + 1) * length)
                mixed_ref[here, cols] = lax.dot_general(
                    weights[here], mixing[n], nn, preferred_element_type=jnp.float32
                ).astype(jnp.bfloat16)
        acc_ref[...] += lax.dot_general(
            mixed_ref[...], buf_ref[3], nt, preferred_element_type=jnp.float32
        )

    @pl.when(step == pieces)
    def _():
        enc_ref[...] = acc_ref[...].astype(jnp.bfloat16)

    @pl.when(step >= pieces)
    def _():
        assemble(wc_refs, place_ref, buf_ref, 4, 1)
        out_ref[0] = lax.dot_general(
            enc_ref[...], buf_ref[4], nn, preferred_element_type=jnp.float32
        ).astype(jnp.bfloat16)


def encoder(place, xs, bias, emb, gain, hit, cond, weights, my_units, length, cond_len):
    pieces, rows, columns = emb.shape
    width = pieces * columns
    last = pieces - 1
    full = lambda shape: pl.BlockSpec(shape, lambda i, p, x: (0,) * len(shape))
    specs = {"a": [], "o": [], "c": []}
    arrays = {"a": [], "o": [], "c": []}
    for kind, array, height, index in weights:
        pick = (
            (lambda i: jnp.minimum(i, last)) if kind in "ao" else (lambda i: jnp.maximum(i - pieces, 0))
        )
        specs[kind].append(
            pl.BlockSpec(
                (None, array.shape[1], height, columns),
                lambda i, p, x, pick=pick, index=index: (pick(i), 0, index, 0),
            )
        )
        arrays[kind].append(array)
    parts = len(specs["a"])
    return pl.pallas_call(
        functools.partial(encoder_body, parts, my_units, length, cond_len),
        out_shape=jax.ShapeDtypeStruct((pieces, rows, columns), jnp.bfloat16),
        grid_spec=pltpu.PrefetchScalarGridSpec(
            num_scalar_prefetch=2,
            grid=(2 * pieces,),
            in_specs=[
                pl.BlockSpec(memory_space=pltpu.SMEM),
                full(emb.shape),
                full(gain.shape),
                full(hit.shape),
                pl.BlockSpec(
                    (1,) + cond.shape[1:], lambda i, p, x: (x[jnp.minimum(i, last)], 0, 0)
                ),
                *specs["a"],
                *specs["o"],
                *specs["c"],
            ],
            out_specs=pl.BlockSpec(
                (1, rows, columns), lambda i, p, x: (jnp.maximum(i - pieces, 0), 0, 0)
            ),
            scratch_shapes=[
                pltpu.VMEM((rows, width), jnp.bfloat16),
                pltpu.VMEM((rows, width), jnp.float32),
                pltpu.VMEM((rows, width), jnp.bfloat16),
                pltpu.VMEM((rows, columns), jnp.bfloat16),
                pltpu.VMEM((5, width, columns), jnp.bfloat16),
            ],
        ),
        compiler_params=pltpu.CompilerParams(
            dimension_semantics=("arbitrary",), vmem_limit_bytes=48 * 1024 * 1024
        ),
        name="encoder",
    )(place, xs, bias, emb, gain, hit, cond, *arrays["a"], *arrays["o"], *arrays["c"])


def attend_body(heads, group, allowed_ref, q_ref, cur_ref, prev_ref, carried_ref, out_ref):
    step = pl.program_id(0)
    nt = (((1,), (1,)), ((), ()))
    nn = (((1,), (0,)), ((), ()))
    tokens = q_ref.shape[0] // group
    key_rows = cur_ref.shape[0] // group
    row = lax.broadcasted_iota(jnp.int32, (tokens, HD), 0)

    def mix(query, kv):
        scores = (
            lax.dot_general(query, kv[:, :HD], nt, preferred_element_type=jnp.float32) * SCALE
        )
        e = jnp.exp(scores - jnp.max(scores, axis=1, keepdims=True))
        weights = (e * (1.0 / jnp.sum(e, axis=1, keepdims=True))).astype(jnp.bfloat16)
        return lax.dot_general(weights, kv[:, HD:], nn, preferred_element_type=jnp.float32)

    for b in range(group):
        here = pl.ds(b * tokens, tokens)
        if b:
            previous = cur_ref[pl.ds((b - 1) * key_rows, key_rows), :]
        else:
            previous = jnp.where(step == 0, carried_ref[...], prev_ref[...])
        query = jnp.concatenate([q_ref[here, pl.ds(h * HD, HD)] for h in range(heads)], axis=0)
        leading = mix(query, previous)
        leading = jnp.where(
            allowed_ref[step * group + b] > 0, leading, jnp.zeros_like(leading)
        )
        tail = pl.ds((b + 1) * tokens - 8, 8)
        final = jnp.concatenate(
            [q_ref[tail, pl.ds(h * HD, HD)].astype(jnp.float32)[7:8] for h in range(heads)], axis=0
        ).astype(jnp.bfloat16)
        trailing = mix(final, cur_ref[pl.ds(b * key_rows, key_rows), :])
        for h in range(heads):
            out_ref[here, pl.ds(h * HD, HD)] = jnp.where(
                row == tokens - 1,
                jnp.broadcast_to(trailing[h : h + 1], (tokens, HD)),
                leading[h * tokens : (h + 1) * tokens],
            ).astype(jnp.bfloat16)


def attend(allowed, queries, keys_values, carried, key_rows):
    block_count = allowed.shape[0]
    group = GROUP
    tokens = queries.shape[0] // block_count
    heads = queries.shape[1] // HD
    return pl.pallas_call(
        functools.partial(attend_body, heads, group),
        out_shape=jax.ShapeDtypeStruct(queries.shape, jnp.bfloat16),
        grid=(block_count // group,),
        in_specs=[
            pl.BlockSpec(memory_space=pltpu.SMEM),
            pl.BlockSpec((group * tokens, queries.shape[1]), lambda c: (c, 0)),
            pl.BlockSpec((group * key_rows, 2 * HD), lambda c: (c, 0)),
            pl.BlockSpec((key_rows, 2 * HD), lambda c: (jnp.maximum(group * c - 1, 0), 0)),
            pl.BlockSpec((key_rows, 2 * HD), lambda c: (0, 0)),
        ],
        out_specs=pl.BlockSpec((group * tokens, queries.shape[1]), lambda c: (c, 0)),
        compiler_params=pltpu.CompilerParams(dimension_semantics=("arbitrary",)),
        name="attend",
    )(allowed, queries, keys_values, keys_values, carried)


def parts(
    db_tokens,
    db_parent,
    db_depth,
    nb_rows,
    seq_start,
    table,
    depth_table,
    enc_gain,
    enc_qkv,
    tree_bias,
    enc_wo,
    cond_kv,
    queries,
    cca_kv,
):
    seq_size = math.prod(lax.axis_size(axis) for axis in SEQ)
    tp_size = lax.axis_size("tp")
    here = lax.axis_index("tp")
    block_count, pair_count = nb_rows.shape
    unit_count = block_count * pair_count
    stored, length = db_tokens.shape
    columns = table.shape[1]
    rows_here = enc_qkv.shape[0]
    kv_cols = cca_kv.shape[2]
    cond_len = cond_kv.shape[0] // block_count
    my_units = unit_count // tp_size
    my_tokens = cond_kv.shape[0] // tp_size
    key_rows = pair_count * length

    flat_rows = nb_rows.reshape(unit_count)
    holder = flat_rows // stored
    local_row = flat_rows % stored
    places = jnp.arange(seq_size, dtype=jnp.int32)
    request = jnp.sum(
        jnp.where(holder[None, :] == places[:, None], local_row[None, :], 0), axis=1
    )
    request = jnp.broadcast_to(request[:, None], (seq_size, 16))

    share = jnp.concatenate(
        [
            enc_qkv.transpose(1, 0, 2).reshape(3 * rows_here, columns),
            enc_wo.T,
            cca_kv.reshape(rows_here, columns),
        ],
        axis=0,
    )[None]
    share = doubled(share, "z", 4)
    share = jnp.concatenate([share] + [moved(share, "z", d) for d in TURNS[1:]], axis=0)
    wanted = exchange(request, SEQ)[:, 0]
    reply = jnp.concatenate(
        [
            jnp.take(db_tokens, wanted, axis=0),
            jnp.take(db_depth, wanted, axis=0),
            jnp.take(db_parent, wanted, axis=0),
        ],
        axis=1,
    )
    reply, pieces_here = lax.optimization_barrier(
        (reply, cond_kv.reshape(tp_size, my_tokens, 2 * columns))
    )
    fetched = exchange(reply, SEQ)
    z_count = lax.axis_size("z")
    shares = lax.all_gather(
        share.reshape(z_count * 5 * rows_here, columns), ("tp", "y", "core"), axis=0
    ).reshape(tp_size, seq_size, 5 * rows_here, columns)
    cond = jnp.stack(
        [lax.dynamic_index_in_dim(pieces_here, here, 0, keepdims=False)]
        + [
            moved(
                lax.dynamic_index_in_dim(pieces_here, (here + d) % tp_size, 0, keepdims=False),
                "tp",
                d,
            )
            for d in range(1, tp_size)
        ]
    )
    fetched = jnp.take(fetched, holder, axis=0)
    tokens = fetched[:, :length].reshape(unit_count * length)
    depths = fetched[:, length : 2 * length].reshape(unit_count * length)
    parents = fetched[:, 2 * length :]
    depth_hit = (
        depths[:, None] == jnp.arange(depth_table.shape[0], dtype=jnp.int32)[None, :]
    ).astype(jnp.bfloat16)
    embedded = (
        jnp.take(table, tokens, axis=0).astype(jnp.float32)
        + jnp.dot(depth_hit, depth_table, preferred_element_type=jnp.float32)
    ).astype(jnp.bfloat16)
    pieces = exchange(embedded.reshape(tp_size, my_units * length, columns), "tp")
    slot = jnp.arange(seq_size, dtype=jnp.int32)
    turn = jnp.array(TURNS, jnp.int32)[slot % z_count // 2]
    z_of = (lax.axis_index("z") + (z_count // 2) * (slot % 2) - turn) % z_count
    place = (z_of * (seq_size // z_count) + slot // z_count)[None]
    parents = lax.dynamic_slice_in_dim(parents, here * my_units, my_units)
    parent_hit = (
        parents.reshape(my_units * length)[:, None] == jnp.arange(length, dtype=parents.dtype)[None, :]
    ).astype(jnp.bfloat16)
    outgoing = encoder(
        place,
        (here - jnp.arange(tp_size, dtype=jnp.int32)) % tp_size,
        tree_bias,
        pieces,
        enc_gain[None],
        parent_hit,
        cond,
        [("a", shares, 3 * SHARE, 0), ("o", shares, SHARE, 3), ("c", shares, SHARE, 4)],
        my_units,
        length,
        cond_len,
    )
    keys_values = exchange(outgoing, "tp").reshape(unit_count * length, 2 * kv_cols)
    carried = lax.ppermute(
        keys_values[(block_count - 1) * key_rows :], SEQ, [(s, s + 1) for s in range(seq_size - 1)]
    )
    block_index = lax.axis_index(SEQ) * block_count + jnp.arange(block_count, dtype=jnp.int32)
    allowed = (block_index > 0) & (seq_start == 0)
    return attend(allowed.astype(jnp.int32), queries, keys_values, carried, key_rows)


def solution(mesh):
    split = Mesh(
        mesh.devices.reshape(8, 4, 2, mesh.shape["tp"]),
        SEQ + ("tp",),
    )
    in_specs = (
        P(SEQ, None),
        P(SEQ, None),
        P(SEQ, None),
        P(SEQ, None),
        P(SEQ),
        P(None, "tp"),
        P(None, "tp"),
        P(),
        P(SEQ, None, "tp"),
        P(),
        P("tp", SEQ),
        P(SEQ, None, "tp"),
        P(SEQ, "tp"),
        P(SEQ, None, "tp"),
    )
    out_specs = P(SEQ, "tp")
    return jax.shard_map(parts, mesh=split, in_specs=in_specs, out_specs=out_specs, check_vma=False)
```

```python
import functools
import math

import jax
import jax.numpy as jnp
from jax import lax
from jax.experimental import pallas as pl
from jax.experimental.pallas import tpu as pltpu
from jax.sharding import Mesh, PartitionSpec as P

HD = 128
SHARE = 16
GROUP = 4
SCALE = 1.0 / math.sqrt(HD)


SEQ = ("z", "y", "core")
TURNS = (0, 1, -1, 2)


def exchange(value, axis):
    return lax.all_to_all(value, axis, split_axis=0, concat_axis=0, tiled=True)


def moved(value, axis, steps):
    count = lax.axis_size(axis)
    return lax.ppermute(value, axis, [(i, (i + steps) % count) for i in range(count)])


def swapped(value, axis, distance):
    count = lax.axis_size(axis)
    return lax.ppermute(value, axis, [(i, i ^ distance) for i in range(count)])


def doubled(value, axis, distance):
    return jnp.concatenate([value, swapped(value, axis, distance)], axis=0)


def assemble(refs, place_ref, target, first, count):
    for r, ref in enumerate(refs):
        slots = ref.shape[0]

        def copy(slot, carry, ref=ref, r=r):
            row = pl.multiple_of(place_ref[r, slot] * SHARE, SHARE)
            for a in range(count):
                target[first + a, pl.ds(row, SHARE), :] = ref[slot, pl.ds(a * SHARE, SHARE), :]
            return carry

        lax.fori_loop(0, slots, copy, 0, unroll=8)


def encoder_body(
    parts, my_units, length, cond_len, place_ref, xs_ref, bias_ref, emb_ref, gain_ref, hit_ref, cond_ref, *refs
):
    wa_refs, wo_refs, wc_refs = refs[:parts], refs[parts : 2 * parts], refs[2 * parts : 3 * parts]
    out_ref, normed_ref, acc_ref, enc_ref, mixed_ref, buf_ref = refs[3 * parts :]
    step = pl.program_id(0)
    pieces, rows, columns = emb_ref.shape
    width = pieces * columns
    nt = (((1,), (1,)), ((), ()))
    nn = (((1,), (0,)), ((), ()))

    @pl.when(step == 0)
    def _():
        for n in range(my_units):
            here = pl.ds(n * length, length)
            value = jnp.concatenate(
                [emb_ref[t, here, :].astype(jnp.float32) for t in range(pieces)], axis=1
            )
            acc_ref[here, :] = value
            mean = jnp.sum(value * value, axis=1, keepdims=True) * (1.0 / width)
            normed_ref[here, :] = (value * lax.rsqrt(mean + 1e-05) * gain_ref[...]).astype(jnp.bfloat16)

    @pl.when(step < pieces)
    def _():
        head = step * (columns // HD)
        assemble(wa_refs, place_ref, buf_ref, 0, 3)
        assemble(wo_refs, place_ref, buf_ref, 3, 1)
        normed = normed_ref[...]
        project = lambda a: lax.dot_general(
            normed, buf_ref[a], nn, preferred_element_type=jnp.float32
        ).astype(jnp.bfloat16)
        query, key, value = project(0), project(1), project(2)
        hit = hit_ref[...].astype(jnp.float32)
        per_block = rows // (cond_ref.shape[1] // cond_len)
        for h in range(columns // HD):
            cols = slice(h * HD, (h + 1) * HD)
            scores, mixing = [], []
            for n in range(my_units):
                here = slice(n * length, (n + 1) * length)
                cond_rows = pl.ds(n * length // per_block * cond_len, cond_len)
                cond_key = cond_ref[0, cond_rows, pl.ds(h * HD, HD)]
                cond_value = cond_ref[0, cond_rows, pl.ds(columns + h * HD, HD)]
                keys = jnp.concatenate([key[here, cols], cond_key, cond_key], axis=0)
                mixing.append(jnp.concatenate([value[here, cols], cond_value, cond_value], axis=0))
                scores.append(
                    lax.dot_general(query[here, cols], keys, nt, preferred_element_type=jnp.float32)
                )
            scores = jnp.concatenate(scores, axis=0) * SCALE
            self_scores = scores[:, :length] + bias_ref[head + h] * hit
            cond_scores = scores[:, length:]
            top = jnp.max(jnp.maximum(self_scores, cond_scores), axis=1, keepdims=True)
            self_e = jnp.exp(self_scores - top)
            cond_e = 0.5 * jnp.exp(cond_scores - top)
            inverse = 1.0 / jnp.sum(self_e + cond_e, axis=1, keepdims=True)
            weights = jnp.concatenate([self_e * inverse, cond_e * inverse], axis=1).astype(jnp.bfloat16)
            for n in range(my_units):
                here = slice(n * length, (n + 1) * length)
                mixed_ref[here, cols] = lax.dot_general(
                    weights[here], mixing[n], nn, preferred_element_type=jnp.float32
                ).astype(jnp.bfloat16)
        acc_ref[...] += lax.dot_general(
            mixed_ref[...], buf_ref[3], nt, preferred_element_type=jnp.float32
        )

    @pl.when(step == pieces)
    def _():
        enc_ref[...] = acc_ref[...].astype(jnp.bfloat16)

    @pl.when(step >= pieces)
    def _():
        assemble(wc_refs, place_ref, buf_ref, 4, 1)
        out_ref[0] = lax.dot_general(
            enc_ref[...], buf_ref[4], nn, preferred_element_type=jnp.float32
        ).astype(jnp.bfloat16)


def encoder(place, xs, bias, emb, gain, hit, cond, weights, my_units, length, cond_len):
    pieces, rows, columns = emb.shape
    width = pieces * columns
    last = pieces - 1
    full = lambda shape: pl.BlockSpec(shape, lambda i, p, x: (0,) * len(shape))
    specs = {"a": [], "o": [], "c": []}
    arrays = {"a": [], "o": [], "c": []}
    for kind, array, height, index in weights:
        pick = (
            (lambda i: jnp.minimum(i, last)) if kind in "ao" else (lambda i: jnp.maximum(i - pieces, 0))
        )
        specs[kind].append(
            pl.BlockSpec(
                (None, array.shape[1], height, columns),
                lambda i, p, x, pick=pick, index=index: (pick(i), 0, index, 0),
            )
        )
        arrays[kind].append(array)
    parts = len(specs["a"])
    return pl.pallas_call(
        functools.partial(encoder_body, parts, my_units, length, cond_len),
        out_shape=jax.ShapeDtypeStruct((pieces, rows, columns), jnp.bfloat16),
        grid_spec=pltpu.PrefetchScalarGridSpec(
            num_scalar_prefetch=2,
            grid=(2 * pieces,),
            in_specs=[
                pl.BlockSpec(memory_space=pltpu.SMEM),
                full(emb.shape),
                full(gain.shape),
                full(hit.shape),
                pl.BlockSpec(
                    (1,) + cond.shape[1:], lambda i, p, x: (x[jnp.minimum(i, last)], 0, 0)
                ),
                *specs["a"],
                *specs["o"],
                *specs["c"],
            ],
            out_specs=pl.BlockSpec(
                (1, rows, columns), lambda i, p, x: (jnp.maximum(i - pieces, 0), 0, 0)
            ),
            scratch_shapes=[
                pltpu.VMEM((rows, width), jnp.bfloat16),
                pltpu.VMEM((rows, width), jnp.float32),
                pltpu.VMEM((rows, width), jnp.bfloat16),
                pltpu.VMEM((rows, columns), jnp.bfloat16),
                pltpu.VMEM((5, width, columns), jnp.bfloat16),
            ],
        ),
        compiler_params=pltpu.CompilerParams(
            dimension_semantics=("arbitrary",), vmem_limit_bytes=48 * 1024 * 1024
        ),
        name="encoder",
    )(place, xs, bias, emb, gain, hit, cond, *arrays["a"], *arrays["o"], *arrays["c"])


def attend_body(heads, group, allowed_ref, q_ref, cur_ref, prev_ref, carried_ref, out_ref):
    step = pl.program_id(0)
    nt = (((1,), (1,)), ((), ()))
    nn = (((1,), (0,)), ((), ()))
    tokens = q_ref.shape[0] // group
    key_rows = cur_ref.shape[0] // group
    row = lax.broadcasted_iota(jnp.int32, (tokens, HD), 0)

    def mix(query, kv):
        scores = (
            lax.dot_general(query, kv[:, :HD], nt, preferred_element_type=jnp.float32) * SCALE
        )
        e = jnp.exp(scores - jnp.max(scores, axis=1, keepdims=True))
        weights = (e * (1.0 / jnp.sum(e, axis=1, keepdims=True))).astype(jnp.bfloat16)
        return lax.dot_general(weights, kv[:, HD:], nn, preferred_element_type=jnp.float32)

    for b in range(group):
        here = pl.ds(b * tokens, tokens)
        if b:
            previous = cur_ref[pl.ds((b - 1) * key_rows, key_rows), :]
        else:
            previous = jnp.where(step == 0, carried_ref[...], prev_ref[...])
        query = jnp.concatenate([q_ref[here, pl.ds(h * HD, HD)] for h in range(heads)], axis=0)
        leading = mix(query, previous)
        leading = jnp.where(
            allowed_ref[step * group + b] > 0, leading, jnp.zeros_like(leading)
        )
        tail = pl.ds((b + 1) * tokens - 8, 8)
        final = jnp.concatenate(
            [q_ref[tail, pl.ds(h * HD, HD)].astype(jnp.float32)[7:8] for h in range(heads)], axis=0
        ).astype(jnp.bfloat16)
        trailing = mix(final, cur_ref[pl.ds(b * key_rows, key_rows), :])
        for h in range(heads):
            out_ref[here, pl.ds(h * HD, HD)] = jnp.where(
                row == tokens - 1,
                jnp.broadcast_to(trailing[h : h + 1], (tokens, HD)),
                leading[h * tokens : (h + 1) * tokens],
            ).astype(jnp.bfloat16)


def attend(allowed, queries, keys_values, carried, key_rows):
    block_count = allowed.shape[0]
    group = GROUP
    tokens = queries.shape[0] // block_count
    heads = queries.shape[1] // HD
    return pl.pallas_call(
        functools.partial(attend_body, heads, group),
        out_shape=jax.ShapeDtypeStruct(queries.shape, jnp.bfloat16),
        grid=(block_count // group,),
        in_specs=[
            pl.BlockSpec(memory_space=pltpu.SMEM),
            pl.BlockSpec((group * tokens, queries.shape[1]), lambda c: (c, 0)),
            pl.BlockSpec((group * key_rows, 2 * HD), lambda c: (c, 0)),
            pl.BlockSpec((key_rows, 2 * HD), lambda c: (jnp.maximum(group * c - 1, 0), 0)),
            pl.BlockSpec((key_rows, 2 * HD), lambda c: (0, 0)),
        ],
        out_specs=pl.BlockSpec((group * tokens, queries.shape[1]), lambda c: (c, 0)),
        compiler_params=pltpu.CompilerParams(dimension_semantics=("arbitrary",)),
        name="attend",
    )(allowed, queries, keys_values, keys_values, carried)


def parts(
    db_tokens,
    db_parent,
    db_depth,
    nb_rows,
    seq_start,
    table,
    depth_table,
    enc_gain,
    enc_qkv,
    tree_bias,
    enc_wo,
    cond_kv,
    queries,
    cca_kv,
):
    seq_size = math.prod(lax.axis_size(axis) for axis in SEQ)
    tp_size = lax.axis_size("tp")
    here = lax.axis_index("tp")
    block_count, pair_count = nb_rows.shape
    unit_count = block_count * pair_count
    stored, length = db_tokens.shape
    columns = table.shape[1]
    rows_here = enc_qkv.shape[0]
    kv_cols = cca_kv.shape[2]
    cond_len = cond_kv.shape[0] // block_count
    my_units = unit_count // tp_size
    my_tokens = cond_kv.shape[0] // tp_size
    key_rows = pair_count * length

    flat_rows = nb_rows.reshape(unit_count)
    holder = flat_rows // stored
    local_row = flat_rows % stored
    places = jnp.arange(seq_size, dtype=jnp.int32)
    request = jnp.sum(
        jnp.where(holder[None, :] == places[:, None], local_row[None, :], 0), axis=1
    )
    request = jnp.broadcast_to(request[:, None], (seq_size, 16))

    share = jnp.concatenate(
        [
            enc_qkv.transpose(1, 0, 2).reshape(3 * rows_here, columns),
            enc_wo.T,
            cca_kv.reshape(rows_here, columns),
        ],
        axis=0,
    )
    share = doubled(share, "z", 4)
    share = jnp.concatenate([share] + [moved(share, "z", d) for d in TURNS[1:]], axis=0)
    wanted = exchange(request, SEQ)[:, 0]
    reply = jnp.concatenate(
        [
            jnp.take(db_tokens, wanted, axis=0),
            jnp.take(db_depth, wanted, axis=0),
            jnp.take(db_parent, wanted, axis=0),
        ],
        axis=1,
    )
    pieces_here = cond_kv.reshape(tp_size, my_tokens, 2 * columns)
    fetched = exchange(reply, SEQ)
    z_count = lax.axis_size("z")
    shares = lax.all_gather(share, ("tp", "y", "core"), axis=0).reshape(
        tp_size, seq_size, 5 * rows_here, columns
    )
    cond = jnp.stack(
        [lax.dynamic_index_in_dim(pieces_here, here, 0, keepdims=False)]
        + [
            moved(
                lax.dynamic_index_in_dim(pieces_here, (here + d) % tp_size, 0, keepdims=False),
                "tp",
                d,
            )
            for d in range(1, tp_size)
        ]
    )
    fetched = jnp.take(fetched, holder, axis=0)
    tokens = fetched[:, :length].reshape(unit_count * length)
    depths = fetched[:, length : 2 * length].reshape(unit_count * length)
    parents = fetched[:, 2 * length :]
    depth_hit = (
        depths[:, None] == jnp.arange(depth_table.shape[0], dtype=jnp.int32)[None, :]
    ).astype(jnp.bfloat16)
    embedded = (
        jnp.take(table, tokens, axis=0).astype(jnp.float32)
        + jnp.dot(depth_hit, depth_table, preferred_element_type=jnp.float32)
    ).astype(jnp.bfloat16)
    pieces = exchange(embedded.reshape(tp_size, my_units * length, columns), "tp")
    slot = jnp.arange(seq_size, dtype=jnp.int32)
    turn = jnp.array(TURNS, jnp.int32)[slot % z_count // 2]
    z_of = (lax.axis_index("z") + (z_count // 2) * (slot % 2) - turn) % z_count
    place = (z_of * (seq_size // z_count) + slot // z_count)[None]
    parents = lax.dynamic_slice_in_dim(parents, here * my_units, my_units)
    parent_hit = (
        parents.reshape(my_units * length)[:, None] == jnp.arange(length, dtype=parents.dtype)[None, :]
    ).astype(jnp.bfloat16)
    outgoing = encoder(
        place,
        (here - jnp.arange(tp_size, dtype=jnp.int32)) % tp_size,
        tree_bias,
        pieces,
        enc_gain[None],
        parent_hit,
        cond,
        [("a", shares, 3 * SHARE, 0), ("o", shares, SHARE, 3), ("c", shares, SHARE, 4)],
        my_units,
        length,
        cond_len,
    )
    keys_values = exchange(outgoing, "tp").reshape(unit_count * length, 2 * kv_cols)
    carried = lax.ppermute(
        keys_values[(block_count - 1) * key_rows :], SEQ, [(s, s + 1) for s in range(seq_size - 1)]
    )
    block_index = lax.axis_index(SEQ) * block_count + jnp.arange(block_count, dtype=jnp.int32)
    allowed = (block_index > 0) & (seq_start == 0)
    return attend(allowed.astype(jnp.int32), queries, keys_values, carried, key_rows)


def solution(mesh):
    split = Mesh(
        mesh.devices.reshape(8, 4, 2, mesh.shape["tp"]),
        SEQ + ("tp",),
    )
    in_specs = (
        P(SEQ, None),
        P(SEQ, None),
        P(SEQ, None),
        P(SEQ, None),
        P(SEQ),
        P(None, "tp"),
        P(None, "tp"),
        P(),
        P(SEQ, None, "tp"),
        P(),
        P("tp", SEQ),
        P(SEQ, None, "tp"),
        P(SEQ, "tp"),
        P(SEQ, None, "tp"),
    )
    out_specs = P(SEQ, "tp")
    return jax.shard_map(parts, mesh=split, in_specs=in_specs, out_specs=out_specs, check_vma=False)
```

```python
import functools
import math

import jax
import jax.numpy as jnp
from jax import lax
from jax.experimental import pallas as pl
from jax.experimental.pallas import tpu as pltpu
from jax.sharding import Mesh, PartitionSpec as P

HD = 128
SHARE = 16
GROUP = 4
SCALE = 1.0 / math.sqrt(HD)


SEQ = ("z", "y", "core")
TURNS = (0, 1, -1, 2)


def exchange(value, axis):
    return lax.all_to_all(value, axis, split_axis=0, concat_axis=0, tiled=True)


def moved(value, axis, steps):
    count = lax.axis_size(axis)
    return lax.ppermute(value, axis, [(i, (i + steps) % count) for i in range(count)])


def swapped(value, axis, distance):
    count = lax.axis_size(axis)
    return lax.ppermute(value, axis, [(i, i ^ distance) for i in range(count)])


def doubled(value, axis, distance):
    return jnp.concatenate([value, swapped(value, axis, distance)], axis=0)


def assemble(refs, place_ref, target, first, count):
    for r, ref in enumerate(refs):
        slots = ref.shape[0]

        def copy(slot, carry, ref=ref, r=r):
            row = pl.multiple_of(place_ref[r, slot] * SHARE, SHARE)
            for a in range(count):
                target[first + a, pl.ds(row, SHARE), :] = ref[slot, pl.ds(a * SHARE, SHARE), :]
            return carry

        lax.fori_loop(0, slots, copy, 0, unroll=8)


def encoder_body(
    parts, my_units, length, cond_len, place_ref, xs_ref, bias_ref, emb_ref, gain_ref, hit_ref, cond_ref, *refs
):
    wa_refs, wo_refs, wc_refs = refs[:parts], refs[parts : 2 * parts], refs[2 * parts : 3 * parts]
    out_ref, normed_ref, acc_ref, enc_ref, mixed_ref, buf_ref = refs[3 * parts :]
    step = pl.program_id(0)
    pieces, rows, columns = emb_ref.shape
    width = pieces * columns
    nt = (((1,), (1,)), ((), ()))
    nn = (((1,), (0,)), ((), ()))

    @pl.when(step == 0)
    def _():
        for n in range(my_units):
            here = pl.ds(n * length, length)
            value = jnp.concatenate(
                [emb_ref[t, here, :].astype(jnp.float32) for t in range(pieces)], axis=1
            )
            acc_ref[here, :] = value
            mean = jnp.sum(value * value, axis=1, keepdims=True) * (1.0 / width)
            normed_ref[here, :] = (value * lax.rsqrt(mean + 1e-05) * gain_ref[...]).astype(jnp.bfloat16)

    @pl.when(step < pieces)
    def _():
        head = step * (columns // HD)
        assemble(wa_refs, place_ref, buf_ref, 0, 3)
        assemble(wo_refs, place_ref, buf_ref, 3, 1)
        normed = normed_ref[...]
        project = lambda a: lax.dot_general(
            normed, buf_ref[a], nn, preferred_element_type=jnp.float32
        ).astype(jnp.bfloat16)
        query, key, value = project(0), project(1), project(2)
        hit = hit_ref[...].astype(jnp.float32)
        per_block = rows // (cond_ref.shape[1] // cond_len)
        for h in range(columns // HD):
            cols = slice(h * HD, (h + 1) * HD)
            scores, mixing = [], []
            for n in range(my_units):
                here = slice(n * length, (n + 1) * length)
                cond_rows = pl.ds(n * length // per_block * cond_len, cond_len)
                cond_key = cond_ref[0, cond_rows, pl.ds(h * HD, HD)]
                cond_value = cond_ref[0, cond_rows, pl.ds(columns + h * HD, HD)]
                keys = jnp.concatenate([key[here, cols], cond_key, cond_key], axis=0)
                mixing.append(jnp.concatenate([value[here, cols], cond_value, cond_value], axis=0))
                scores.append(
                    lax.dot_general(query[here, cols], keys, nt, preferred_element_type=jnp.float32)
                )
            scores = jnp.concatenate(scores, axis=0) * SCALE
            self_scores = scores[:, :length] + bias_ref[head + h] * hit
            cond_scores = scores[:, length:]
            top = jnp.max(jnp.maximum(self_scores, cond_scores), axis=1, keepdims=True)
            self_e = jnp.exp(self_scores - top)
            cond_e = 0.5 * jnp.exp(cond_scores - top)
            inverse = 1.0 / jnp.sum(self_e + cond_e, axis=1, keepdims=True)
            weights = jnp.concatenate([self_e * inverse, cond_e * inverse], axis=1).astype(jnp.bfloat16)
            for n in range(my_units):
                here = slice(n * length, (n + 1) * length)
                mixed_ref[here, cols] = lax.dot_general(
                    weights[here], mixing[n], nn, preferred_element_type=jnp.float32
                ).astype(jnp.bfloat16)
        acc_ref[...] += lax.dot_general(
            mixed_ref[...], buf_ref[3], nt, preferred_element_type=jnp.float32
        )

    @pl.when(step == pieces)
    def _():
        enc_ref[...] = acc_ref[...].astype(jnp.bfloat16)

    @pl.when(step >= pieces)
    def _():
        assemble(wc_refs, place_ref, buf_ref, 4, 1)
        out_ref[0] = lax.dot_general(
            enc_ref[...], buf_ref[4], nn, preferred_element_type=jnp.float32
        ).astype(jnp.bfloat16)


def encoder(place, xs, bias, emb, gain, hit, cond, weights, my_units, length, cond_len):
    pieces, rows, columns = emb.shape
    width = pieces * columns
    last = pieces - 1
    full = lambda shape: pl.BlockSpec(shape, lambda i, p, x: (0,) * len(shape))
    specs = {"a": [], "o": [], "c": []}
    arrays = {"a": [], "o": [], "c": []}
    for kind, array, height, index in weights:
        pick = (
            (lambda i: jnp.minimum(i, last)) if kind in "ao" else (lambda i: jnp.maximum(i - pieces, 0))
        )
        specs[kind].append(
            pl.BlockSpec(
                (None, array.shape[1], height, columns),
                lambda i, p, x, pick=pick, index=index: (pick(i), 0, index, 0),
            )
        )
        arrays[kind].append(array)
    parts = len(specs["a"])
    return pl.pallas_call(
        functools.partial(encoder_body, parts, my_units, length, cond_len),
        out_shape=jax.ShapeDtypeStruct((pieces, rows, columns), jnp.bfloat16),
        grid_spec=pltpu.PrefetchScalarGridSpec(
            num_scalar_prefetch=2,
            grid=(2 * pieces,),
            in_specs=[
                pl.BlockSpec(memory_space=pltpu.SMEM),
                full(emb.shape),
                full(gain.shape),
                full(hit.shape),
                pl.BlockSpec(
                    (1,) + cond.shape[1:], lambda i, p, x: (x[jnp.minimum(i, last)], 0, 0)
                ),
                *specs["a"],
                *specs["o"],
                *specs["c"],
            ],
            out_specs=pl.BlockSpec(
                (1, rows, columns), lambda i, p, x: (jnp.maximum(i - pieces, 0), 0, 0)
            ),
            scratch_shapes=[
                pltpu.VMEM((rows, width), jnp.bfloat16),
                pltpu.VMEM((rows, width), jnp.float32),
                pltpu.VMEM((rows, width), jnp.bfloat16),
                pltpu.VMEM((rows, columns), jnp.bfloat16),
                pltpu.VMEM((5, width, columns), jnp.bfloat16),
            ],
        ),
        compiler_params=pltpu.CompilerParams(
            dimension_semantics=("arbitrary",), vmem_limit_bytes=48 * 1024 * 1024
        ),
        name="encoder",
    )(place, xs, bias, emb, gain, hit, cond, *arrays["a"], *arrays["o"], *arrays["c"])


def attend_body(heads, group, allowed_ref, q_ref, cur_ref, prev_ref, carried_ref, out_ref):
    step = pl.program_id(0)
    nt = (((1,), (1,)), ((), ()))
    nn = (((1,), (0,)), ((), ()))
    tokens = q_ref.shape[0] // group
    key_rows = cur_ref.shape[0] // group
    row = lax.broadcasted_iota(jnp.int32, (tokens, HD), 0)

    def mix(query, kv):
        scores = (
            lax.dot_general(query, kv[:, :HD], nt, preferred_element_type=jnp.float32) * SCALE
        )
        e = jnp.exp(scores - jnp.max(scores, axis=1, keepdims=True))
        weights = (e * (1.0 / jnp.sum(e, axis=1, keepdims=True))).astype(jnp.bfloat16)
        return lax.dot_general(weights, kv[:, HD:], nn, preferred_element_type=jnp.float32)

    for b in range(group):
        here = pl.ds(b * tokens, tokens)
        if b:
            previous = cur_ref[pl.ds((b - 1) * key_rows, key_rows), :]
        else:
            previous = jnp.where(step == 0, carried_ref[...], prev_ref[...])
        query = jnp.concatenate([q_ref[here, pl.ds(h * HD, HD)] for h in range(heads)], axis=0)
        leading = mix(query, previous)
        leading = jnp.where(
            allowed_ref[step * group + b] > 0, leading, jnp.zeros_like(leading)
        )
        tail = pl.ds((b + 1) * tokens - 8, 8)
        final = jnp.concatenate(
            [q_ref[tail, pl.ds(h * HD, HD)].astype(jnp.float32)[7:8] for h in range(heads)], axis=0
        ).astype(jnp.bfloat16)
        trailing = mix(final, cur_ref[pl.ds(b * key_rows, key_rows), :])
        for h in range(heads):
            out_ref[here, pl.ds(h * HD, HD)] = jnp.where(
                row == tokens - 1,
                jnp.broadcast_to(trailing[h : h + 1], (tokens, HD)),
                leading[h * tokens : (h + 1) * tokens],
            ).astype(jnp.bfloat16)


def attend(allowed, queries, keys_values, carried, key_rows):
    block_count = allowed.shape[0]
    group = GROUP
    tokens = queries.shape[0] // block_count
    heads = queries.shape[1] // HD
    return pl.pallas_call(
        functools.partial(attend_body, heads, group),
        out_shape=jax.ShapeDtypeStruct(queries.shape, jnp.bfloat16),
        grid=(block_count // group,),
        in_specs=[
            pl.BlockSpec(memory_space=pltpu.SMEM),
            pl.BlockSpec((group * tokens, queries.shape[1]), lambda c: (c, 0)),
            pl.BlockSpec((group * key_rows, 2 * HD), lambda c: (c, 0)),
            pl.BlockSpec((key_rows, 2 * HD), lambda c: (jnp.maximum(group * c - 1, 0), 0)),
            pl.BlockSpec((key_rows, 2 * HD), lambda c: (0, 0)),
        ],
        out_specs=pl.BlockSpec((group * tokens, queries.shape[1]), lambda c: (c, 0)),
        compiler_params=pltpu.CompilerParams(dimension_semantics=("arbitrary",)),
        name="attend",
    )(allowed, queries, keys_values, keys_values, carried)


def parts(
    db_tokens,
    db_parent,
    db_depth,
    nb_rows,
    seq_start,
    table,
    depth_table,
    enc_gain,
    enc_qkv,
    tree_bias,
    enc_wo,
    cond_kv,
    queries,
    cca_kv,
):
    seq_size = math.prod(lax.axis_size(axis) for axis in SEQ)
    tp_size = lax.axis_size("tp")
    here = lax.axis_index("tp")
    block_count, pair_count = nb_rows.shape
    unit_count = block_count * pair_count
    stored, length = db_tokens.shape
    columns = table.shape[1]
    rows_here = enc_qkv.shape[0]
    kv_cols = cca_kv.shape[2]
    cond_len = cond_kv.shape[0] // block_count
    my_units = unit_count // tp_size
    my_tokens = cond_kv.shape[0] // tp_size
    key_rows = pair_count * length

    flat_rows = nb_rows.reshape(unit_count)
    holder = flat_rows // stored
    local_row = flat_rows % stored
    places = jnp.arange(seq_size, dtype=jnp.int32)
    request = jnp.sum(
        jnp.where(holder[None, :] == places[:, None], local_row[None, :], 0), axis=1
    )
    request = jnp.broadcast_to(request[:, None], (seq_size, 16))

    share = jnp.concatenate(
        [
            enc_qkv.transpose(1, 0, 2).reshape(3 * rows_here, columns),
            enc_wo.T,
            cca_kv.reshape(rows_here, columns),
        ],
        axis=0,
    )
    share = doubled(share, "z", 4)
    share, request = lax.optimization_barrier((share, request))
    share = jnp.concatenate([share] + [moved(share, "z", d) for d in TURNS[1:]], axis=0)
    wanted = exchange(request, SEQ)[:, 0]
    reply = jnp.concatenate(
        [
            jnp.take(db_tokens, wanted, axis=0),
            jnp.take(db_depth, wanted, axis=0),
            jnp.take(db_parent, wanted, axis=0),
        ],
        axis=1,
    )
    reply, pieces_here = lax.optimization_barrier(
        (reply, cond_kv.reshape(tp_size, my_tokens, 2 * columns))
    )
    fetched = exchange(reply, SEQ)
    z_count = lax.axis_size("z")
    shares = lax.all_gather(share, ("tp", "y", "core"), axis=0).reshape(
        tp_size, seq_size, 5 * rows_here, columns
    )
    cond = jnp.stack(
        [lax.dynamic_index_in_dim(pieces_here, here, 0, keepdims=False)]
        + [
            moved(
                lax.dynamic_index_in_dim(pieces_here, (here + d) % tp_size, 0, keepdims=False),
                "tp",
                d,
            )
            for d in range(1, tp_size)
        ]
    )
    fetched, cond = lax.optimization_barrier((fetched, cond))
    fetched = jnp.take(fetched, holder, axis=0)
    tokens = fetched[:, :length].reshape(unit_count * length)
    depths = fetched[:, length : 2 * length].reshape(unit_count * length)
    parents = fetched[:, 2 * length :]
    depth_hit = (
        depths[:, None] == jnp.arange(depth_table.shape[0], dtype=jnp.int32)[None, :]
    ).astype(jnp.bfloat16)
    embedded = (
        jnp.take(table, tokens, axis=0).astype(jnp.float32)
        + jnp.dot(depth_hit, depth_table, preferred_element_type=jnp.float32)
    ).astype(jnp.bfloat16)
    pieces = exchange(embedded.reshape(tp_size, my_units * length, columns), "tp")
    slot = jnp.arange(seq_size, dtype=jnp.int32)
    turn = jnp.array(TURNS, jnp.int32)[slot % z_count // 2]
    z_of = (lax.axis_index("z") + (z_count // 2) * (slot % 2) - turn) % z_count
    place = (z_of * (seq_size // z_count) + slot // z_count)[None]
    parents = lax.dynamic_slice_in_dim(parents, here * my_units, my_units)
    parent_hit = (
        parents.reshape(my_units * length)[:, None] == jnp.arange(length, dtype=parents.dtype)[None, :]
    ).astype(jnp.bfloat16)
    outgoing = encoder(
        place,
        (here - jnp.arange(tp_size, dtype=jnp.int32)) % tp_size,
        tree_bias,
        pieces,
        enc_gain[None],
        parent_hit,
        cond,
        [("a", shares, 3 * SHARE, 0), ("o", shares, SHARE, 3), ("c", shares, SHARE, 4)],
        my_units,
        length,
        cond_len,
    )
    keys_values = exchange(outgoing, "tp").reshape(unit_count * length, 2 * kv_cols)
    carried = lax.ppermute(
        keys_values[(block_count - 1) * key_rows :], SEQ, [(s, s + 1) for s in range(seq_size - 1)]
    )
    block_index = lax.axis_index(SEQ) * block_count + jnp.arange(block_count, dtype=jnp.int32)
    allowed = (block_index > 0) & (seq_start == 0)
    return attend(allowed.astype(jnp.int32), queries, keys_values, carried, key_rows)


def solution(mesh):
    split = Mesh(
        mesh.devices.reshape(8, 4, 2, mesh.shape["tp"]),
        SEQ + ("tp",),
    )
    in_specs = (
        P(SEQ, None),
        P(SEQ, None),
        P(SEQ, None),
        P(SEQ, None),
        P(SEQ),
        P(None, "tp"),
        P(None, "tp"),
        P(),
        P(SEQ, None, "tp"),
        P(),
        P("tp", SEQ),
        P(SEQ, None, "tp"),
        P(SEQ, "tp"),
        P(SEQ, None, "tp"),
    )
    out_specs = P(SEQ, "tp")
    return jax.shard_map(parts, mesh=split, in_specs=in_specs, out_specs=out_specs, check_vma=False)
```

```python
import functools
import math

import jax
import jax.numpy as jnp
from jax import lax
from jax.experimental import pallas as pl
from jax.experimental.pallas import tpu as pltpu
from jax.sharding import Mesh, PartitionSpec as P

HD = 128
SHARE = 16
GROUP = 4
SCALE = 1.0 / math.sqrt(HD)


SEQ = ("z", "y", "core")
TURNS = (0, 1, -1, 2)


def exchange(value, axis):
    return lax.all_to_all(value, axis, split_axis=0, concat_axis=0, tiled=True)


def moved(value, axis, steps):
    count = lax.axis_size(axis)
    return lax.ppermute(value, axis, [(i, (i + steps) % count) for i in range(count)])


def swapped(value, axis, distance):
    count = lax.axis_size(axis)
    return lax.ppermute(value, axis, [(i, i ^ distance) for i in range(count)])


def doubled(value, axis, distance):
    return jnp.concatenate([value, swapped(value, axis, distance)], axis=0)


def assemble(refs, place_ref, target, first, count):
    for r, ref in enumerate(refs):
        slots = ref.shape[0]

        def copy(slot, carry, ref=ref, r=r):
            row = pl.multiple_of(place_ref[r, slot] * SHARE, SHARE)
            for a in range(count):
                target[first + a, pl.ds(row, SHARE), :] = ref[slot, pl.ds(a * SHARE, SHARE), :]
            return carry

        lax.fori_loop(0, slots, copy, 0, unroll=8)


def encoder_body(
    parts, my_units, length, cond_len, place_ref, xs_ref, bias_ref, emb_ref, gain_ref, hit_ref, cond_ref, *refs
):
    wa_refs, wo_refs, wc_refs = refs[:parts], refs[parts : 2 * parts], refs[2 * parts : 3 * parts]
    out_ref, normed_ref, acc_ref, enc_ref, mixed_ref, buf_ref = refs[3 * parts :]
    step = pl.program_id(0)
    pieces, rows, columns = emb_ref.shape
    width = pieces * columns
    nt = (((1,), (1,)), ((), ()))
    nn = (((1,), (0,)), ((), ()))

    @pl.when(step == 0)
    def _():
        for n in range(my_units):
            here = pl.ds(n * length, length)
            value = jnp.concatenate(
                [emb_ref[t, here, :].astype(jnp.float32) for t in range(pieces)], axis=1
            )
            acc_ref[here, :] = value
            mean = jnp.sum(value * value, axis=1, keepdims=True) * (1.0 / width)
            normed_ref[here, :] = (value * lax.rsqrt(mean + 1e-05) * gain_ref[...]).astype(jnp.bfloat16)

    @pl.when(step < pieces)
    def _():
        head = step * (columns // HD)
        assemble(wa_refs, place_ref, buf_ref, 0, 3)
        assemble(wo_refs, place_ref, buf_ref, 3, 1)
        normed = normed_ref[...]
        project = lambda a: lax.dot_general(
            normed, buf_ref[a], nn, preferred_element_type=jnp.float32
        ).astype(jnp.bfloat16)
        query, key, value = project(0), project(1), project(2)
        hit = hit_ref[...].astype(jnp.float32)
        per_block = rows // (cond_ref.shape[1] // cond_len)
        for h in range(columns // HD):
            cols = slice(h * HD, (h + 1) * HD)
            scores, mixing = [], []
            for n in range(my_units):
                here = slice(n * length, (n + 1) * length)
                cond_rows = pl.ds(n * length // per_block * cond_len, cond_len)
                cond_key = cond_ref[0, cond_rows, pl.ds(h * HD, HD)]
                cond_value = cond_ref[0, cond_rows, pl.ds(columns + h * HD, HD)]
                keys = jnp.concatenate([key[here, cols], cond_key, cond_key], axis=0)
                mixing.append(jnp.concatenate([value[here, cols], cond_value, cond_value], axis=0))
                scores.append(
                    lax.dot_general(query[here, cols], keys, nt, preferred_element_type=jnp.float32)
                )
            scores = jnp.concatenate(scores, axis=0) * SCALE
            self_scores = scores[:, :length] + bias_ref[head + h] * hit
            cond_scores = scores[:, length:]
            top = jnp.max(jnp.maximum(self_scores, cond_scores), axis=1, keepdims=True)
            self_e = jnp.exp(self_scores - top)
            cond_e = 0.5 * jnp.exp(cond_scores - top)
            inverse = 1.0 / jnp.sum(self_e + cond_e, axis=1, keepdims=True)
            weights = jnp.concatenate([self_e * inverse, cond_e * inverse], axis=1).astype(jnp.bfloat16)
            for n in range(my_units):
                here = slice(n * length, (n + 1) * length)
                mixed_ref[here, cols] = lax.dot_general(
                    weights[here], mixing[n], nn, preferred_element_type=jnp.float32
                ).astype(jnp.bfloat16)
        acc_ref[...] += lax.dot_general(
            mixed_ref[...], buf_ref[3], nt, preferred_element_type=jnp.float32
        )

    @pl.when(step == pieces)
    def _():
        enc_ref[...] = acc_ref[...].astype(jnp.bfloat16)

    @pl.when(step >= pieces)
    def _():
        assemble(wc_refs, place_ref, buf_ref, 4, 1)
        out_ref[0] = lax.dot_general(
            enc_ref[...], buf_ref[4], nn, preferred_element_type=jnp.float32
        ).astype(jnp.bfloat16)


def encoder(place, xs, bias, emb, gain, hit, cond, weights, my_units, length, cond_len):
    pieces, rows, columns = emb.shape
    width = pieces * columns
    last = pieces - 1
    full = lambda shape: pl.BlockSpec(shape, lambda i, p, x: (0,) * len(shape))
    specs = {"a": [], "o": [], "c": []}
    arrays = {"a": [], "o": [], "c": []}
    for kind, array, height, index in weights:
        pick = (
            (lambda i: jnp.minimum(i, last)) if kind in "ao" else (lambda i: jnp.maximum(i - pieces, 0))
        )
        specs[kind].append(
            pl.BlockSpec(
                (None, array.shape[1], height, columns),
                lambda i, p, x, pick=pick, index=index: (pick(i), 0, index, 0),
            )
        )
        arrays[kind].append(array)
    parts = len(specs["a"])
    return pl.pallas_call(
        functools.partial(encoder_body, parts, my_units, length, cond_len),
        out_shape=jax.ShapeDtypeStruct((pieces, rows, columns), jnp.bfloat16),
        grid_spec=pltpu.PrefetchScalarGridSpec(
            num_scalar_prefetch=2,
            grid=(2 * pieces,),
            in_specs=[
                pl.BlockSpec(memory_space=pltpu.SMEM),
                full(emb.shape),
                full(gain.shape),
                full(hit.shape),
                pl.BlockSpec(
                    (1,) + cond.shape[1:], lambda i, p, x: (x[jnp.minimum(i, last)], 0, 0)
                ),
                *specs["a"],
                *specs["o"],
                *specs["c"],
            ],
            out_specs=pl.BlockSpec(
                (1, rows, columns), lambda i, p, x: (jnp.maximum(i - pieces, 0), 0, 0)
            ),
            scratch_shapes=[
                pltpu.VMEM((rows, width), jnp.bfloat16),
                pltpu.VMEM((rows, width), jnp.float32),
                pltpu.VMEM((rows, width), jnp.bfloat16),
                pltpu.VMEM((rows, columns), jnp.bfloat16),
                pltpu.VMEM((5, width, columns), jnp.bfloat16),
            ],
        ),
        compiler_params=pltpu.CompilerParams(
            dimension_semantics=("arbitrary",), vmem_limit_bytes=48 * 1024 * 1024
        ),
        name="encoder",
    )(place, xs, bias, emb, gain, hit, cond, *arrays["a"], *arrays["o"], *arrays["c"])


def attend_body(heads, group, allowed_ref, q_ref, cur_ref, prev_ref, carried_ref, out_ref):
    step = pl.program_id(0)
    nt = (((1,), (1,)), ((), ()))
    nn = (((1,), (0,)), ((), ()))
    tokens = q_ref.shape[0] // group
    key_rows = cur_ref.shape[0] // group
    row = lax.broadcasted_iota(jnp.int32, (tokens, HD), 0)

    def mix(query, kv):
        scores = (
            lax.dot_general(query, kv[:, :HD], nt, preferred_element_type=jnp.float32) * SCALE
        )
        e = jnp.exp(scores - jnp.max(scores, axis=1, keepdims=True))
        weights = (e * (1.0 / jnp.sum(e, axis=1, keepdims=True))).astype(jnp.bfloat16)
        return lax.dot_general(weights, kv[:, HD:], nn, preferred_element_type=jnp.float32)

    for b in range(group):
        here = pl.ds(b * tokens, tokens)
        if b:
            previous = cur_ref[pl.ds((b - 1) * key_rows, key_rows), :]
        else:
            previous = jnp.where(step == 0, carried_ref[...], prev_ref[...])
        query = jnp.concatenate([q_ref[here, pl.ds(h * HD, HD)] for h in range(heads)], axis=0)
        leading = mix(query, previous)
        leading = jnp.where(
            allowed_ref[step * group + b] > 0, leading, jnp.zeros_like(leading)
        )
        tail = pl.ds((b + 1) * tokens - 8, 8)
        final = jnp.concatenate(
            [q_ref[tail, pl.ds(h * HD, HD)].astype(jnp.float32)[7:8] for h in range(heads)], axis=0
        ).astype(jnp.bfloat16)
        trailing = mix(final, cur_ref[pl.ds(b * key_rows, key_rows), :])
        for h in range(heads):
            out_ref[here, pl.ds(h * HD, HD)] = jnp.where(
                row == tokens - 1,
                jnp.broadcast_to(trailing[h : h + 1], (tokens, HD)),
                leading[h * tokens : (h + 1) * tokens],
            ).astype(jnp.bfloat16)


def attend(allowed, queries, keys_values, carried, key_rows):
    block_count = allowed.shape[0]
    group = GROUP
    tokens = queries.shape[0] // block_count
    heads = queries.shape[1] // HD
    return pl.pallas_call(
        functools.partial(attend_body, heads, group),
        out_shape=jax.ShapeDtypeStruct(queries.shape, jnp.bfloat16),
        grid=(block_count // group,),
        in_specs=[
            pl.BlockSpec(memory_space=pltpu.SMEM),
            pl.BlockSpec((group * tokens, queries.shape[1]), lambda c: (c, 0)),
            pl.BlockSpec((group * key_rows, 2 * HD), lambda c: (c, 0)),
            pl.BlockSpec((key_rows, 2 * HD), lambda c: (jnp.maximum(group * c - 1, 0), 0)),
            pl.BlockSpec((key_rows, 2 * HD), lambda c: (0, 0)),
        ],
        out_specs=pl.BlockSpec((group * tokens, queries.shape[1]), lambda c: (c, 0)),
        compiler_params=pltpu.CompilerParams(dimension_semantics=("arbitrary",)),
        name="attend",
    )(allowed, queries, keys_values, keys_values, carried)


def parts(
    db_tokens,
    db_parent,
    db_depth,
    nb_rows,
    seq_start,
    table,
    depth_table,
    enc_gain,
    enc_qkv,
    tree_bias,
    enc_wo,
    cond_kv,
    queries,
    cca_kv,
):
    seq_size = math.prod(lax.axis_size(axis) for axis in SEQ)
    tp_size = lax.axis_size("tp")
    here = lax.axis_index("tp")
    block_count, pair_count = nb_rows.shape
    unit_count = block_count * pair_count
    stored, length = db_tokens.shape
    columns = table.shape[1]
    rows_here = enc_qkv.shape[0]
    kv_cols = cca_kv.shape[2]
    cond_len = cond_kv.shape[0] // block_count
    my_units = unit_count // tp_size
    my_tokens = cond_kv.shape[0] // tp_size
    key_rows = pair_count * length

    flat_rows = nb_rows.reshape(unit_count)
    holder = flat_rows // stored
    local_row = flat_rows % stored
    places = jnp.arange(seq_size, dtype=jnp.int32)
    request = jnp.sum(
        jnp.where(holder[None, :] == places[:, None], local_row[None, :], 0), axis=1
    )
    request = jnp.broadcast_to(request[:, None], (seq_size, 16))

    share = jnp.concatenate(
        [
            enc_qkv.transpose(1, 0, 2).reshape(3 * rows_here, columns),
            enc_wo.T,
            cca_kv.reshape(rows_here, columns),
        ],
        axis=0,
    )
    share = doubled(share, "z", 4)
    share, request = lax.optimization_barrier((share, request))
    share = jnp.concatenate([share] + [moved(share, "z", d) for d in TURNS[1:]], axis=0)
    wanted = exchange(request, SEQ)[:, 0]
    stacked = jnp.concatenate([db_tokens, db_depth, db_parent], axis=1)
    reply = jnp.take(stacked, wanted, axis=0, mode="clip")
    reply, pieces_here = lax.optimization_barrier(
        (reply, cond_kv.reshape(tp_size, my_tokens, 2 * columns))
    )
    fetched = exchange(reply, SEQ)
    z_count = lax.axis_size("z")
    shares = lax.all_gather(share, ("tp", "y", "core"), axis=0).reshape(
        tp_size, seq_size, 5 * rows_here, columns
    )
    cond = jnp.stack(
        [lax.dynamic_index_in_dim(pieces_here, here, 0, keepdims=False)]
        + [
            moved(
                lax.dynamic_index_in_dim(pieces_here, (here + d) % tp_size, 0, keepdims=False),
                "tp",
                d,
            )
            for d in range(1, tp_size)
        ]
    )
    fetched = jnp.take(fetched, holder, axis=0, mode="clip")
    tokens = fetched[:, :length].reshape(unit_count * length)
    depths = fetched[:, length : 2 * length].reshape(unit_count * length)
    parents = fetched[:, 2 * length :]
    depth_hit = (
        depths[:, None] == jnp.arange(depth_table.shape[0], dtype=jnp.int32)[None, :]
    ).astype(jnp.bfloat16)
    embedded = (
        jnp.take(table, tokens, axis=0, mode="clip").astype(jnp.float32)
        + jnp.dot(depth_hit, depth_table, preferred_element_type=jnp.float32)
    ).astype(jnp.bfloat16)
    pieces = exchange(embedded.reshape(tp_size, my_units * length, columns), "tp")
    slot = jnp.arange(seq_size, dtype=jnp.int32)
    turn = jnp.array(TURNS, jnp.int32)[slot % z_count // 2]
    z_of = (lax.axis_index("z") + (z_count // 2) * (slot % 2) - turn) % z_count
    place = (z_of * (seq_size // z_count) + slot // z_count)[None]
    parents = lax.dynamic_slice_in_dim(parents, here * my_units, my_units)
    parent_hit = (
        parents.reshape(my_units * length)[:, None] == jnp.arange(length, dtype=parents.dtype)[None, :]
    ).astype(jnp.bfloat16)
    outgoing = encoder(
        place,
        (here - jnp.arange(tp_size, dtype=jnp.int32)) % tp_size,
        tree_bias,
        pieces,
        enc_gain[None],
        parent_hit,
        cond,
        [("a", shares, 3 * SHARE, 0), ("o", shares, SHARE, 3), ("c", shares, SHARE, 4)],
        my_units,
        length,
        cond_len,
    )
    keys_values = exchange(outgoing, "tp").reshape(unit_count * length, 2 * kv_cols)
    carried = lax.ppermute(
        keys_values[(block_count - 1) * key_rows :], SEQ, [(s, s + 1) for s in range(seq_size - 1)]
    )
    block_index = lax.axis_index(SEQ) * block_count + jnp.arange(block_count, dtype=jnp.int32)
    allowed = (block_index > 0) & (seq_start == 0)
    return attend(allowed.astype(jnp.int32), queries, keys_values, carried, key_rows)


def solution(mesh):
    split = Mesh(
        mesh.devices.reshape(8, 4, 2, mesh.shape["tp"]),
        SEQ + ("tp",),
    )
    in_specs = (
        P(SEQ, None),
        P(SEQ, None),
        P(SEQ, None),
        P(SEQ, None),
        P(SEQ),
        P(None, "tp"),
        P(None, "tp"),
        P(),
        P(SEQ, None, "tp"),
        P(),
        P("tp", SEQ),
        P(SEQ, None, "tp"),
        P(SEQ, "tp"),
        P(SEQ, None, "tp"),
    )
    out_specs = P(SEQ, "tp")
    return jax.shard_map(parts, mesh=split, in_specs=in_specs, out_specs=out_specs, check_vma=False)
```
